32 devices in a mesh: groups: 2 (over y), seq: 16 (over z, x, core).
Axes of the slice: x: 2, y: 2, z: 4, core: 2. Of those that a mesh axis runs over, the one named last changes fastest.
Arguments:
- queries: bfloat16 [32, 16384], P(('groups', 'seq')), parts along dimension 0, may hold values from -8 to 8
- prompt_keys: bfloat16 [8192, 1024], P(('groups', 'seq')), parts along dimension 0, may hold values from -16 to 16
- prompt_values: bfloat16 [8192, 1024], P(('groups', 'seq')), parts along dimension 0, may hold values from -6 to 6
- suffix_keys: bfloat16 [32, 8, 64, 1024], P(('groups', 'seq')), parts along dimension 0, may hold values from -16 to 16
- suffix_values: bfloat16 [32, 8, 64, 1024], P(('groups', 'seq')), parts along dimension 0, may hold values from -6 to 6
- suffix_lengths: int32 [32], P(('groups', 'seq')), parts along dimension 0, may hold values from 1 to 512, 5120 in all
- block_tables: int32 [32, 8], P(('groups', 'seq')), parts along dimension 0, may hold values from 0 to 7, each once within a row
Outputs:
- attended: bfloat16 [32, 16384], P(('groups', 'seq')), parts along dimension 0
The draws below stay inside these ranges and needn't reach their ends.
There are 2 independent parts, one for each index of `groups`. The reference program is written for one: setup_inputs(seed, part) draws one part's arguments, and reference() takes and returns one part's arrays. A program takes and returns all parts, laid end to end along the dimension named above; each array names one. Nothing has to cross between parts.
Inputs may be any that keep to these rules, and one draw needn't show every extreme that they name: `suffix_lengths`: in each group, one sample has exactly 512 live suffix positions, and the lengths of the group's 16 samples sum to 5120. `block_tables`: each row names every one of the sample's 8 pages once.
All inputs are finite; a program needn't handle non-finite values.
Results may differ from the reference program's by a relative error of at most 0.0025.
Values may be sent and summed in bfloat16 or wider, within the bound.
A program may use at most 64 MiB of HBM per device.

```python
import math
import jax
import jax.numpy as jnp
import numpy as np
from jax import lax

H = 128
KVH = 8
HD = 128
PROMPT_DEV = 256
PAGE = 64
PAGES = 8
PROMPT = 4096
SAMPLES = 16
SUF_MAX = 512
N_SEQ = 16


def base_queries(key):
    queries = 1.5 * jax.random.normal(jax.random.fold_in(key, 11), (SAMPLES, H * HD), jnp.float32)
    return jnp.clip(queries, -8.0, 8.0)


def full_queries(key):
    queries = base_queries(key)
    return queries


def draw_queries(key, part):
    return full_queries(key).astype(jnp.bfloat16)


def draw_prompt_keys(key, part):
    prompt_keys = 2.0 * jax.random.normal(jax.random.fold_in(key, 17), (PROMPT, KVH * HD), jnp.float32)
    return jnp.clip(prompt_keys, -16.0, 16.0).astype(jnp.bfloat16)


def draw_suffix_keys(key, part):
    queries = full_queries(key).reshape(SAMPLES, KVH, H // KVH, HD)
    group_mean = jnp.mean(queries, axis=2).reshape(SAMPLES, 1, 1, KVH * HD)
    noise = jax.random.normal(jax.random.fold_in(key, 23), (SAMPLES, PAGES, PAGE, KVH * HD), jnp.float32)
    suffix_keys = 2.0 * noise + 4.0 * group_mean
    return jnp.clip(suffix_keys, -16.0, 16.0).astype(jnp.bfloat16)


def levels(rng, dims, pieces, low, largest):
    level, own = 1.0, jax.random.fold_in(rng, 6)
    for position, parts in pieces:
        steps = jnp.exp(jax.random.uniform(jax.random.fold_in(own, position), (parts,), jnp.float32, low / len(pieces), largest / len(pieces)))
        level = level * jnp.repeat(steps, dims[position] // parts).reshape([-1 if axis == position else 1 for axis in range(len(dims))])
    return level


def split_up(count, total, most, lean):
    portions = [(1 << 20) // math.isqrt(rank ** lean) + 1 for rank in range(2, count + 1)]
    spare, given = total - most - (count - 1), [1] * (count - 1)
    while spare > 0:
        candidates = [i for i in range(count - 1) if given[i] < most]
        pool, remaining = sum([portions[i] for i in candidates]), spare
        for i in candidates:
            more = min(most - given[i], max(1, remaining * portions[i] // pool), spare)
            given[i] = given[i] + more
            spare = spare - more
    return np.array([most] + given)


def uneven(own_key, count, total, limit, lean):
    if count == 2:
        one = jax.random.randint(own_key, (), max(1, total - limit), min(limit, total - 1) + 1)
        return jnp.stack([one, total - one])
    sizes = jnp.asarray(split_up(count, total, limit, lean), jnp.int32)
    pairs = (count - 1) // 2
    giver, sink = sizes[1:1 + 2 * pairs:2], sizes[2:2 + 2 * pairs:2]
    slack = jnp.minimum(giver - 1, limit - sink)
    moved = jax.random.randint(jax.random.fold_in(own_key, 1), (pairs,), 0, 1 << 20) % (slack + 1)
    sizes = sizes.at[1:1 + 2 * pairs:2].set(giver - moved).at[2:2 + 2 * pairs:2].set(sink + moved)
    return sizes[jax.random.permutation(jax.random.fold_in(own_key, 2), count)]


def scatter_about(rng, dims, deviation, bound, cuts=(), held_as=jnp.bfloat16):
    entries = deviation * jax.random.normal(rng, dims, jnp.float32)
    if cuts:
        entries = entries * levels(rng, dims, cuts, -0.22, 0.18)
    return jnp.clip(entries, -bound, bound).astype(held_as)


def setup_inputs(seed: int = 0, part: int = 0) -> dict:
    splits = jax.random.split(jax.random.key(seed), 8)
    part_splits = jax.random.split(jax.random.fold_in(splits[7], part), 8)
    queries = draw_queries(jax.random.fold_in(jax.random.fold_in(splits[7], part), 71), part)
    prompt_keys = draw_prompt_keys(jax.random.fold_in(jax.random.fold_in(splits[7], part), 71), part)
    prompt_values = scatter_about(part_splits[2], (PROMPT, KVH * HD), 1.0, 6.0, ((0, 16),))
    suffix_keys = draw_suffix_keys(jax.random.fold_in(jax.random.fold_in(splits[7], part), 71), part)
    suffix_values = scatter_about(part_splits[4], (SAMPLES, PAGES, PAGE, KVH * HD), 1.0, 6.0, ((0, 16),))
    suffix_lengths = uneven(part_splits[5], SAMPLES, SAMPLES * SUF_MAX * 5 // 8, SUF_MAX, 2).astype(jnp.int32)
    block_tables = jax.vmap(lambda own: jax.random.permutation(own, PAGES))(jax.random.split(part_splits[6], SAMPLES)).reshape((SAMPLES, PAGES)).astype(jnp.int32)
    return {"queries": queries, "prompt_keys": prompt_keys, "prompt_values": prompt_values, "suffix_keys": suffix_keys, "suffix_values": suffix_values, "suffix_lengths": suffix_lengths, "block_tables": block_tables}


def prompt_partial(query_heads, key_block, value_block):
    scores = jnp.einsum('skgd,pkd->skgp', query_heads.astype(jnp.float32), key_block.astype(jnp.float32)) * (1.0 / math.sqrt(HD))
    maxima = lax.optimization_barrier(jnp.max(scores, axis=-1))
    expos = jnp.exp(scores - maxima[..., None])
    totals = lax.optimization_barrier(jnp.sum(expos, axis=-1))
    weights = lax.optimization_barrier(expos.astype(jnp.bfloat16))
    numerators = jnp.einsum('skgp,pkd->skgd', weights.astype(jnp.float32), value_block.astype(jnp.float32))
    return (maxima, totals, numerators)

def suffix_partial(query_heads, key_pages, value_pages, live_mask):
    scores = jnp.einsum('skgd,stkd->skgt', query_heads.astype(jnp.float32), key_pages.astype(jnp.float32)) * (1.0 / math.sqrt(HD))
    scores = jnp.where(live_mask[:, None, None, :], scores, -jnp.inf)
    maxima = lax.optimization_barrier(jnp.max(scores, axis=-1))
    expos = jnp.exp(scores - maxima[..., None])
    totals = lax.optimization_barrier(jnp.sum(expos, axis=-1))
    weights = lax.optimization_barrier(expos.astype(jnp.bfloat16))
    numerators = jnp.einsum('skgt,stkd->skgd', weights.astype(jnp.float32), value_pages.astype(jnp.float32))
    return (maxima, totals, numerators)

def reference(queries, prompt_keys, prompt_values, suffix_keys, suffix_values, suffix_lengths, block_tables):
    samples = queries.shape[0]
    per_kv = H // KVH
    query_heads = queries.reshape(samples, KVH, per_kv, HD)
    key_shards = prompt_keys.reshape(N_SEQ, PROMPT_DEV, KVH, HD)
    value_shards = prompt_values.reshape(N_SEQ, PROMPT_DEV, KVH, HD)

    def absorb(carry, shard):
        run_max, run_total, run_num = carry
        maxima, totals, numerators = prompt_partial(query_heads, shard[0], shard[1])
        new_max = jnp.maximum(run_max, maxima)
        old_scale = jnp.exp(run_max - new_max)
        new_scale = jnp.exp(maxima - new_max)
        run_total = run_total * old_scale + totals * new_scale
        run_num = run_num * old_scale[..., None] + numerators * new_scale[..., None]
        return ((new_max, run_total, run_num), None)
    start = (jnp.full((samples, KVH, per_kv), -jnp.inf, jnp.float32), jnp.zeros((samples, KVH, per_kv), jnp.float32), jnp.zeros((samples, KVH, per_kv, HD), jnp.float32))
    carried, _ = lax.scan(absorb, start, (key_shards, value_shards))
    prompt_max, prompt_total, prompt_num = carried
    picker = block_tables.astype(jnp.int32)[:, :, None, None]
    key_pages = jnp.take_along_axis(suffix_keys, picker, axis=1).reshape(samples, PAGES * PAGE, KVH, HD)
    value_pages = jnp.take_along_axis(suffix_values, picker, axis=1).reshape(samples, PAGES * PAGE, KVH, HD)
    live_mask = jnp.arange(PAGES * PAGE, dtype=jnp.int32)[None, :] < suffix_lengths.astype(jnp.int32)[:, None]
    suffix_max, suffix_total, suffix_num = suffix_partial(query_heads, key_pages, value_pages, live_mask)
    overall = jnp.maximum(prompt_max, suffix_max)
    prompt_scale = jnp.exp(prompt_max - overall)
    suffix_scale = jnp.exp(suffix_max - overall)
    numer_sum = prompt_num * prompt_scale[..., None] + suffix_num * suffix_scale[..., None]
    denom_sum = prompt_total * prompt_scale + suffix_total * suffix_scale
    attended = numer_sum / denom_sum[..., None]
    return attended.reshape(samples, H * HD).astype(jnp.bfloat16)
```

```python
import functools
import math

import jax
import jax.numpy as jnp
from jax import lax
from jax.experimental import pallas as pl
from jax.experimental.pallas import tpu as pltpu
from jax.sharding import PartitionSpec as P

H = 128
KVH = 8
HD = 128
G = H // KVH
HALF = H // 2
HK = KVH // 2
LINK = jnp.int16
UNROLL = 16
FULL = 32767.0
SCALE = 1.0 / math.sqrt(HD)
NT = (((1,), (1,)), ((), ()))


def kernel(
    n, q_hbm, k, v, sk, sv, lens_hbm, tables_hbm, out,
    flat_q, lens, tables, q, rows32, qbuf, kbuf, vbuf, skb, svb, osend, orecv, ssend, srecv, osuf, lsuf,
    q_send, q_recv, o_send, o_recv, s_send, s_recv, kv_send, kv_recv, own_sem,
):
    me = lax.axis_index("seq")
    core = lax.rem(me, 2)
    partner = me + 1 - 2 * core
    rows = k.shape[0]
    width = k.shape[1] // 2
    nb = n // 4
    mine = me // 4

    def remote(src, dst, send, recv, peer):
        return pltpu.make_async_remote_copy(
            src_ref=src, dst_ref=dst, send_sem=send, recv_sem=recv,
            device_id={"seq": peer}, device_id_type=pl.DeviceIdType.MESH,
        )

    def each(low, high, step):
        if n <= UNROLL:
            for i in range(low, high):
                step(i)
        else:
            pl.loop(low, high)(step)

    def peer_of(i):
        group = lax.rem(mine + nb - i // 4, nb)
        return group * 4 + lax.rem(me + i, 4)

    barrier = pltpu.get_barrier_semaphore()

    def greet(i):
        pl.semaphore_signal(
            barrier, inc=1, device_id={"seq": peer_of(n - i)},
            device_id_type=pl.DeviceIdType.MESH,
        )

    each(1, n, greet)

    own_cols = pl.ds(pl.multiple_of(core * width, width), width)
    own_half = pl.ds(pl.multiple_of(core * HALF, HALF), HALF)
    local = [
        pltpu.make_async_copy(q_hbm, flat_q, own_sem.at[0]),
        pltpu.make_async_copy(lens_hbm, lens, own_sem.at[1]),
        pltpu.make_async_copy(tables_hbm, tables, own_sem.at[2]),
        pltpu.make_async_copy(sk.at[0], skb, own_sem.at[3]),
        pltpu.make_async_copy(sv.at[0], svb, own_sem.at[4]),
        pltpu.make_async_copy(k.at[:, own_cols], kbuf.at[pl.ds(0, rows)], own_sem.at[5]),
        pltpu.make_async_copy(v.at[:, own_cols], vbuf.at[pl.ds(0, rows)], own_sem.at[6]),
    ]
    for copy in local:
        copy.start()
    local[0].wait()
    for h in range(H):
        rows32[h:h + 1] = flat_q[:, h * HD:(h + 1) * HD].astype(jnp.float32)
    q[...] = rows32[...].astype(jnp.bfloat16)
    qbuf[me] = q[own_half]

    pl.semaphore_wait(barrier, n - 1)

    def q_copy(peer):
        cut = pl.ds(pl.multiple_of(lax.rem(peer, 2) * HALF, HALF), HALF)
        return remote(q.at[cut], qbuf.at[me], q_send.at[peer], q_recv.at[me], peer)

    each(4, n, lambda i: q_copy(peer_of(i)).start())
    each(1, 4, lambda i: q_copy(peer_of(i)).start())

    away_cols = pl.ds(pl.multiple_of((1 - core) * width, width), width)
    kv = [
        remote(k.at[:, away_cols], kbuf.at[pl.ds(rows, rows)], kv_send.at[0], kv_recv.at[0], partner),
        remote(v.at[:, away_cols], vbuf.at[pl.ds(rows, rows)], kv_send.at[1], kv_recv.at[1], partner),
    ]
    for copy in kv:
        copy.start()

    for copy in local[1:5]:
        copy.wait()
    pages, page = skb.shape[0], skb.shape[1]
    slots = pages * page
    lane = lax.broadcasted_iota(jnp.int32, (1, slots), 1)
    at_page = lane // page
    position = lane - at_page * page
    for j in range(pages):
        position = position + jnp.where(at_page == tables[0, j], j * page, 0)
    live = position < lens[0]
    for h in range(KVH):
        cols = pl.ds(h * HD, HD)
        keys = skb[:, :, cols].reshape(slots, HD)
        values = svb[:, :, cols].reshape(slots, HD)
        part = pl.ds(h * G, G)
        scores = lax.dot_general(q[part], keys, NT, preferred_element_type=jnp.float32)
        scores = jnp.where(live, scores, -jnp.inf)
        top = jnp.max(scores, axis=1, keepdims=True)
        expos = jnp.exp((scores - top) * SCALE)
        total = jnp.sum(expos, axis=1, keepdims=True)
        num = jnp.dot(expos.astype(jnp.bfloat16), values, preferred_element_type=jnp.float32)
        osuf[part] = num / total
        lsuf[part] = jnp.broadcast_to(top * SCALE + jnp.log(total), (G, HD))

    for copy in local[5:]:
        copy.wait()
    for copy in kv:
        copy.wait_recv()

    def o_copy(peer):
        return remote(osend.at[peer], orecv.at[me], o_send.at[peer], o_recv.at[me], peer)

    def s_copy(peer):
        return remote(ssend.at[peer], srecv.at[me], s_send.at[peer], s_recv.at[me], peer)

    kept = [
        pltpu.make_async_copy(osend.at[me], orecv.at[me], own_sem.at[7]),
        pltpu.make_async_copy(ssend.at[me], srecv.at[me], own_sem.at[8]),
    ]
    wide = lax.broadcasted_iota(jnp.int32, (G, HD), 1)

    def spread(column):
        tile = jnp.zeros((G, HD), jnp.float32)
        for s in range(4):
            tile = jnp.where(wide == s, column[s * G:(s + 1) * G], tile)
        return tile

    def batch(b):
        group = lax.rem(mine + b, nb)
        for j in range(4):
            source = group * 4 + j

            @pl.when(source != me)
            def _():
                remote(qbuf.at[source], qbuf.at[source], q_send.at[source], q_recv.at[source], partner).wait_recv()

        four = pl.ds(pl.multiple_of(group * 4, 4), 4)
        lses, steps = [], []
        ones = jnp.ones((kbuf.shape[0], HD), jnp.bfloat16)
        for h in range(HK):
            cols = pl.ds(h * HD, HD)
            asked = qbuf[four, pl.ds(h * G, G), :].reshape(4 * G, HD)
            scores = lax.dot_general(asked, kbuf[:, cols], NT, preferred_element_type=jnp.float32)
            top = jnp.max(scores, axis=1, keepdims=True)
            expos = jnp.exp((scores - top) * SCALE)
            wider = jnp.concatenate([vbuf[:, cols], ones], axis=1)
            both = jnp.dot(expos.astype(jnp.bfloat16), wider, preferred_element_type=jnp.float32)
            num, total = both[:, :HD], both[:, HD:]
            peak = jnp.maximum(jnp.max(jnp.abs(num), axis=1, keepdims=True), 1e-30)
            fixed = jnp.round(num * (FULL / peak)).astype(jnp.int32).astype(LINK)
            osend[four, pl.ds(h * G, G), :] = fixed.reshape(4, G, HD)
            lses.append(spread(top * SCALE + jnp.log(total)))
            steps.append(spread(peak / (FULL * total)))
        flat = jnp.concatenate(lses + steps, axis=0).T
        for s in range(4):
            ssend[group * 4 + s] = flat[s:s + 1]
        for j in range(4):
            peer = group * 4 + j

            @pl.when(peer != me)
            def _():
                s_copy(peer).start()
                o_copy(peer).start()

        @pl.when(group == mine)
        def _():
            for copy in kept:
                copy.start()

    each(0, nb, batch)

    def left(i):
        peer = peer_of(i)
        q_copy(peer).wait_send()
        o_copy(peer).wait_send()
        s_copy(peer).wait_send()

    for copy in kv:
        copy.wait_send()
    each(1, n, left)

    order = [lax.rem(mine + i // 4, nb) * 4 + lax.rem(me + i, 4) for i in range(n)]
    kept[1].wait()
    for source in order[1:]:
        remote(ssend.at[source], srecv.at[source], s_send.at[source], s_recv.at[source], partner).wait_recv()
    flat = [srecv[source] for source in order]
    if n % HD:
        flat.append(jnp.zeros((HD - n % HD, HD), jnp.float32))
    turned = jnp.concatenate(flat, axis=0).T
    lse, steps = turned[:HALF], turned[HALF:]
    from_lane = lax.broadcasted_iota(jnp.int32, lse.shape, 1)
    accs, weights = [], []
    for side in range(2):
        half = lax.rem(core + side, 2)
        part = pl.ds(pl.multiple_of(half * HALF, HALF), HALF)
        ok = jnp.logical_and(lax.rem(from_lane, 2) == side, from_lane < n)
        there = jnp.where(ok, lse, -jnp.inf)
        suffix = lsuf[part]
        top = jnp.maximum(jnp.max(there, axis=1, keepdims=True), suffix[:, :1])
        weight = jnp.exp(there - top)
        own = jnp.exp(suffix[:, :1] - top)
        total = jnp.sum(weight, axis=1, keepdims=True) + own
        inverse = 1.0 / total
        weights.append(weight * jnp.where(ok, steps, 0.0) * inverse)
        accs.append(osuf[part] * (own * inverse))
    kept[0].wait()
    for i, source in enumerate(order):
        if i:
            remote(osend.at[source], orecv.at[source], o_send.at[source], o_recv.at[source], partner).wait_recv()
        side = i % 2
        accs[side] = accs[side] + weights[side][:, i:i + 1] * orecv[source].astype(jnp.float32)
    for side in range(2):
        base = lax.rem(core + side, 2) * HALF
        out[pl.ds(pl.multiple_of(base, HALF), HALF)] = accs[side].astype(jnp.bfloat16)


def per_device(n, queries, keys, values, suffix_keys, suffix_values, lengths, tables):
    rows = keys.shape[0]
    pages, page, width = suffix_keys.shape[1:]
    dma = pltpu.SemaphoreType.DMA
    hbm = pl.BlockSpec(memory_space=pltpu.HBM)
    vector = pl.BlockSpec(memory_space=pltpu.VMEM)
    out = pl.pallas_call(
        functools.partial(kernel, n),
        out_shape=pltpu.VMEM((H, HD), jnp.bfloat16),
        in_specs=[hbm] * 7,
        out_specs=vector,
        scratch_shapes=[
            pltpu.VMEM(queries.shape, jnp.bfloat16),
            pltpu.SMEM(lengths.shape, jnp.int32),
            pltpu.SMEM(tables.shape, jnp.int32),
            pltpu.VMEM((H, HD), jnp.bfloat16),
            pltpu.VMEM((H, HD), jnp.float32),
            pltpu.VMEM((n, HALF, HD), jnp.bfloat16),
            pltpu.VMEM((2 * rows, width // 2), jnp.bfloat16),
            pltpu.VMEM((2 * rows, width // 2), jnp.bfloat16),
            pltpu.VMEM((pages, page, width), jnp.bfloat16),
            pltpu.VMEM((pages, page, width), jnp.bfloat16),
            pltpu.VMEM((n, HALF, HD), LINK),
            pltpu.VMEM((n, HALF, HD), LINK),
            pltpu.VMEM((n, 1, HD), jnp.float32),
            pltpu.VMEM((n, 1, HD), jnp.float32),
            pltpu.VMEM((H, HD), jnp.float32),
            pltpu.VMEM((H, HD), jnp.float32),
            dma((n,)), dma((n,)), dma((n,)), dma((n,)), dma((n,)), dma((n,)),
            dma((2,)), dma((2,)), dma((9,)),
        ],
        compiler_params=pltpu.CompilerParams(collective_id=0, has_side_effects=True),
        name="attend",
    )(queries, keys, values, suffix_keys, suffix_values, lengths, tables)
    return out.reshape(1, H * HD)


def solution(mesh):
    rows = P(("groups", "seq"), None)
    pages = P(("groups", "seq"), None, None, None)
    return jax.shard_map(
        functools.partial(per_device, mesh.shape["seq"]),
        mesh=mesh,
        in_specs=(rows, rows, rows, pages, pages, P(("groups", "seq")), rows),
        out_specs=rows,
        check_vma=False,
    )
```

```python
import functools
import math

import jax
import jax.numpy as jnp
from jax import lax
from jax.experimental import pallas as pl
from jax.experimental.pallas import tpu as pltpu
from jax.sharding import PartitionSpec as P

H = 128
KVH = 8
HD = 128
G = H // KVH
HALF = H // 2
HK = KVH // 2
LINK = jnp.int16
UNROLL = 16
FULL = 32767.0
SCALE = 1.0 / math.sqrt(HD)
NT = (((1,), (1,)), ((), ()))


def kernel(
    n, q_hbm, k, v, sk, sv, lens_hbm, tables_hbm, out,
    flat_q, lens, tables, q, rows32, qbuf, kbuf, vbuf, skb, svb, osend, orecv, ssend, srecv, osuf, lsuf, spread_w,
    q_send, q_recv, o_send, o_recv, s_send, s_recv, kv_send, kv_recv, own_sem, ready, paired,
):
    me = lax.axis_index("seq")
    core = lax.rem(me, 2)
    partner = me + 1 - 2 * core
    rows = k.shape[0]
    width = k.shape[1] // 2
    nb = n // 4
    mine = me // 4

    def remote(src, dst, send, recv, peer):
        return pltpu.make_async_remote_copy(
            src_ref=src, dst_ref=dst, send_sem=send, recv_sem=recv,
            device_id={"seq": peer}, device_id_type=pl.DeviceIdType.MESH,
        )

    def signal(semaphore, peer):
        pl.semaphore_signal(
            semaphore, inc=1, device_id={"seq": peer}, device_id_type=pl.DeviceIdType.MESH
        )

    def each(low, high, step):
        if n <= UNROLL:
            for i in range(low, high):
                step(i)
        else:
            pl.loop(low, high)(step)

    own_cols = pl.ds(pl.multiple_of(core * width, width), width)
    own_half = pl.ds(pl.multiple_of(core * HALF, HALF), HALF)
    local = [
        pltpu.make_async_copy(q_hbm, flat_q, own_sem.at[0]),
        pltpu.make_async_copy(lens_hbm, lens, own_sem.at[1]),
        pltpu.make_async_copy(tables_hbm, tables, own_sem.at[2]),
        pltpu.make_async_copy(sk.at[0], skb, own_sem.at[3]),
        pltpu.make_async_copy(sv.at[0], svb, own_sem.at[4]),
        pltpu.make_async_copy(k.at[:, own_cols], kbuf.at[pl.ds(0, rows)], own_sem.at[5]),
        pltpu.make_async_copy(v.at[:, own_cols], vbuf.at[pl.ds(0, rows)], own_sem.at[6]),
    ]
    local[0].start()
    barrier = pltpu.get_barrier_semaphore()

    def greet(peer):
        @pl.when(peer > me)
        def _():
            signal(barrier, peer)

    each(1, n, greet)
    for copy in local[1:]:
        copy.start()

    @pl.when(me > 0)
    def _():
        pl.semaphore_wait(barrier, me)

    def answer(peer):
        @pl.when(peer < me)
        def _():
            signal(ready.at[mine], peer)

    each(0, n - 1, answer)

    @pl.when(core == 1)
    def _():
        signal(paired, partner)
    local[0].wait()
    for h in range(H):
        rows32[h:h + 1] = flat_q[:, h * HD:(h + 1) * HD].astype(jnp.float32)
    q[...] = rows32[...].astype(jnp.bfloat16)
    qbuf[me] = q[own_half]

    def q_copy(peer):
        cut = pl.ds(pl.multiple_of(lax.rem(peer, 2) * HALF, HALF), HALF)
        return remote(q.at[cut], qbuf.at[me], q_send.at[peer], q_recv.at[me], peer)

    away_cols = pl.ds(pl.multiple_of((1 - core) * width, width), width)
    kv = [
        remote(k.at[:, away_cols], kbuf.at[pl.ds(rows, rows)], kv_send.at[0], kv_recv.at[0], partner),
        remote(v.at[:, away_cols], vbuf.at[pl.ds(rows, rows)], kv_send.at[1], kv_recv.at[1], partner),
    ]

    def ask(group):
        @pl.when(group > mine)
        def _():
            pl.semaphore_wait(ready.at[group], 4)

        @pl.when(jnp.logical_and(group == mine, lax.rem(me, 4) < 3))
        def _():
            pl.semaphore_wait(ready.at[group], 3 - lax.rem(me, 4))

        for j in range(4):
            peer = group * 4 + j

            @pl.when(peer != me)
            def _():
                q_copy(peer).start()

    pages, page = skb.shape[0], skb.shape[1]
    slots = pages * page

    def suffix(low, high):
        lane = lax.broadcasted_iota(jnp.int32, (1, slots), 1)
        at_page = lane // page
        position = lane - at_page * page
        for j in range(pages):
            position = position + jnp.where(at_page == tables[0, j], j * page, 0)
        live = position < lens[0]
        for h in range(low, high):
            cols = pl.ds(h * HD, HD)
            keys = skb[:, :, cols].reshape(slots, HD)
            values = svb[:, :, cols].reshape(slots, HD)
            part = pl.ds(h * G, G)
            scores = lax.dot_general(q[part], keys, NT, preferred_element_type=jnp.float32)
            scores = jnp.where(live, scores, -jnp.inf)
            top = jnp.max(scores, axis=1, keepdims=True)
            expos = jnp.exp((scores - top) * SCALE)
            total = jnp.sum(expos, axis=1, keepdims=True)
            num = jnp.dot(expos.astype(jnp.bfloat16), values, preferred_element_type=jnp.float32)
            osuf[part] = num / total
            lsuf[part] = jnp.broadcast_to(top * SCALE + jnp.log(total), (G, HD))

    @pl.when(core == 0)
    def _():
        pl.semaphore_wait(paired, 1)

    for copy in kv:
        copy.start()
    for group in range(4):
        ask(group)
    if nb > 4:
        pl.loop(4, nb)(ask)
    for copy in local[1:5]:
        copy.wait()
    suffix(0, KVH)
    lsuf[...] = lsuf[...].T

    for copy in local[5:]:
        copy.wait()
    for copy in kv:
        copy.wait_recv()

    def o_copy(peer):
        return remote(osend.at[peer], orecv.at[me], o_send.at[peer], o_recv.at[me], peer)

    def s_copy(peer):
        return remote(ssend.at[peer], srecv.at[me], s_send.at[peer], s_recv.at[me], peer)

    kept = [
        pltpu.make_async_copy(osend.at[me], orecv.at[me], own_sem.at[7]),
        pltpu.make_async_copy(ssend.at[me], srecv.at[me], own_sem.at[8]),
    ]
    wide = lax.broadcasted_iota(jnp.int32, (G, HD), 1)

    def spread(column):
        tile = jnp.zeros((G, HD), jnp.float32)
        for s in range(4):
            tile = jnp.where(wide == s, column[s * G:(s + 1) * G], tile)
        return tile

    def turn(b):
        return b + 0

    def batch(b):
        group = turn(b)
        for j in range(4):
            source = group * 4 + j

            @pl.when(source != me)
            def _():
                remote(qbuf.at[source], qbuf.at[source], q_send.at[source], q_recv.at[source], partner).wait_recv()

        four = pl.ds(pl.multiple_of(group * 4, 4), 4)
        lses, steps = [], []
        ones = jnp.ones((kbuf.shape[0], HD), jnp.bfloat16)
        for h in range(HK):
            cols = pl.ds(h * HD, HD)
            asked = qbuf[four, pl.ds(h * G, G), :].reshape(4 * G, HD)
            scores = lax.dot_general(asked, kbuf[:, cols], NT, preferred_element_type=jnp.float32)
            top = jnp.max(scores, axis=1, keepdims=True)
            expos = jnp.exp((scores - top) * SCALE)
            wider = jnp.concatenate([vbuf[:, cols], ones], axis=1)
            both = jnp.dot(expos.astype(jnp.bfloat16), wider, preferred_element_type=jnp.float32)
            num, total = both[:, :HD], both[:, HD:]
            peak = jnp.maximum(jnp.max(jnp.abs(num), axis=1, keepdims=True), 1e-30)
            fixed = jnp.round(num * (FULL / peak)).astype(jnp.int32).astype(LINK)
            osend[four, pl.ds(h * G, G), :] = fixed.reshape(4, G, HD)
            lses.append(spread(top * SCALE + jnp.log(total)))
            steps.append(spread(peak / (FULL * total)))
        flat = jnp.concatenate(lses + steps, axis=0).T
        for s in range(4):
            ssend[group * 4 + s] = flat[s:s + 1]
        for j in range(4):
            peer = group * 4 + j

            @pl.when(peer != me)
            def _():
                s_copy(peer).start()
                o_copy(peer).start()

        @pl.when(group == mine)
        def _():
            for copy in kept:
                copy.start()

    each(0, nb, batch)

    def s_wait(source):
        @pl.when(source != me)
        def _():
            remote(ssend.at[source], srecv.at[source], s_send.at[source], s_recv.at[source], partner).wait_recv()

    kept[1].wait()
    each(0, n, s_wait)
    lanes = lax.broadcasted_iota(jnp.int32, (n // 2, HD), 1) < HALF
    even = jnp.concatenate([srecv[i] for i in range(0, n, 2)], axis=0)
    odd = jnp.concatenate([srecv[i] for i in range(1, n, 2)], axis=0)
    lse = jnp.where(lanes, even, pltpu.roll(odd, HALF, 1))
    steps = jnp.where(lanes, pltpu.roll(even, HALF, 1), odd)
    suffix_lse = lsuf[0:1]
    top = jnp.maximum(jnp.max(lse, axis=0, keepdims=True), suffix_lse)
    weight = jnp.exp(lse - top)
    own = jnp.exp(suffix_lse - top)
    inverse = 1.0 / (jnp.sum(weight, axis=0, keepdims=True) + own)
    flat = [weight * steps * inverse, own * inverse]
    flat.append(jnp.zeros((HD - (n // 2 + 1) % HD, HD), jnp.float32))
    turned = jnp.concatenate(flat, axis=0).T
    for i in range(n // 2):
        spread_w[i] = jnp.broadcast_to(turned[:, i:i + 1], (H, HD))
    acc = osuf[...] * turned[:, n // 2:n // 2 + 1]
    kept[0].wait()
    for b in range(nb):
        group = turn(b)
        for j in range(4):
            source = group * 4 + j

            @pl.when(source != me)
            def _():
                remote(osend.at[source], orecv.at[source], o_send.at[source], o_recv.at[source], partner).wait_recv()

        for chip in range(2):
            both = pl.ds(pl.multiple_of(group * 4 + chip * 2, 2), 2)
            acc = acc + spread_w[group * 2 + chip] * orecv[both].reshape(H, HD).astype(jnp.float32)
    out[...] = acc.astype(jnp.bfloat16)

    for copy in kv:
        copy.wait_send()

    def left(peer):
        @pl.when(peer != me)
        def _():
            q_copy(peer).wait_send()
            o_copy(peer).wait_send()
            s_copy(peer).wait_send()

    each(0, n, left)


def per_device(n, queries, keys, values, suffix_keys, suffix_values, lengths, tables):
    rows = keys.shape[0]
    pages, page, width = suffix_keys.shape[1:]
    dma = pltpu.SemaphoreType.DMA
    hbm = pl.BlockSpec(memory_space=pltpu.HBM)
    vector = pl.BlockSpec(memory_space=pltpu.VMEM)
    out = pl.pallas_call(
        functools.partial(kernel, n),
        out_shape=pltpu.VMEM((H, HD), jnp.bfloat16),
        in_specs=[hbm] * 7,
        out_specs=vector,
        scratch_shapes=[
            pltpu.VMEM(queries.shape, jnp.bfloat16),
            pltpu.SMEM(lengths.shape, jnp.int32),
            pltpu.SMEM(tables.shape, jnp.int32),
            pltpu.VMEM((H, HD), jnp.bfloat16),
            pltpu.VMEM((H, HD), jnp.float32),
            pltpu.VMEM((n, HALF, HD), jnp.bfloat16),
            pltpu.VMEM((2 * rows, width // 2), jnp.bfloat16),
            pltpu.VMEM((2 * rows, width // 2), jnp.bfloat16),
            pltpu.VMEM((pages, page, width), jnp.bfloat16),
            pltpu.VMEM((pages, page, width), jnp.bfloat16),
            pltpu.VMEM((n, HALF, HD), LINK),
            pltpu.VMEM((n, HALF, HD), LINK),
            pltpu.VMEM((n, 1, HD), jnp.float32),
            pltpu.VMEM((n, 1, HD), jnp.float32),
            pltpu.VMEM((H, HD), jnp.float32),
            pltpu.VMEM((H, HD), jnp.float32),
            pltpu.VMEM((n // 2, H, HD), jnp.float32),
            dma((n,)), dma((n,)), dma((n,)), dma((n,)), dma((n,)), dma((n,)),
            dma((2,)), dma((2,)), dma((9,)),
            pltpu.SemaphoreType.REGULAR((n // 4,)),
            pltpu.SemaphoreType.REGULAR,
        ],
        compiler_params=pltpu.CompilerParams(collective_id=0, has_side_effects=True),
        name="attend",
    )(queries, keys, values, suffix_keys, suffix_values, lengths, tables)
    return out.reshape(1, H * HD)


def solution(mesh):
    rows = P(("groups", "seq"), None)
    pages = P(("groups", "seq"), None, None, None)
    return jax.shard_map(
        functools.partial(per_device, mesh.shape["seq"]),
        mesh=mesh,
        in_specs=(rows, rows, rows, pages, pages, P(("groups", "seq")), rows),
        out_specs=rows,
        check_vma=False,
    )
```

```python
import functools
import math

import jax
import jax.numpy as jnp
from jax import lax
from jax.experimental import pallas as pl
from jax.experimental.pallas import tpu as pltpu
from jax.sharding import PartitionSpec as P

H = 128
KVH = 8
HD = 128
G = H // KVH
HALF = H // 2
HK = KVH // 2
LINK = jnp.int16
UNROLL = 16
FULL = 32767.0
SCALE = 1.0 / math.sqrt(HD)
NT = (((1,), (1,)), ((), ()))


def kernel(
    n, q_hbm, k, v, sk, sv, lens_hbm, tables_hbm, out,
    flat_q, lens, tables, q, rows32, qbuf, kbuf, vbuf, skb, svb, osend, orecv, ssend, srecv, osuf, lsuf,
    q_send, q_recv, o_send, o_recv, s_send, s_recv, kv_send, kv_recv, own_sem, ready, paired,
):
    me = lax.axis_index("seq")
    core = lax.rem(me, 2)
    partner = me + 1 - 2 * core
    rows = k.shape[0]
    width = k.shape[1] // 2
    nb = n // 4
    mine = me // 4

    def remote(src, dst, send, recv, peer):
        return pltpu.make_async_remote_copy(
            src_ref=src, dst_ref=dst, send_sem=send, recv_sem=recv,
            device_id={"seq": peer}, device_id_type=pl.DeviceIdType.MESH,
        )

    def signal(semaphore, peer):
        pl.semaphore_signal(
            semaphore, inc=1, device_id={"seq": peer}, device_id_type=pl.DeviceIdType.MESH
        )

    def each(low, high, step):
        if n <= UNROLL:
            for i in range(low, high):
                step(i)
        else:
            pl.loop(low, high)(step)

    own_cols = pl.ds(pl.multiple_of(core * width, width), width)
    own_half = pl.ds(pl.multiple_of(core * HALF, HALF), HALF)
    local = [
        pltpu.make_async_copy(q_hbm, flat_q, own_sem.at[0]),
        pltpu.make_async_copy(lens_hbm, lens, own_sem.at[1]),
        pltpu.make_async_copy(tables_hbm, tables, own_sem.at[2]),
        pltpu.make_async_copy(sk.at[0], skb, own_sem.at[3]),
        pltpu.make_async_copy(sv.at[0], svb, own_sem.at[4]),
        pltpu.make_async_copy(k.at[:, own_cols], kbuf.at[pl.ds(0, rows)], own_sem.at[5]),
        pltpu.make_async_copy(v.at[:, own_cols], vbuf.at[pl.ds(0, rows)], own_sem.at[6]),
    ]
    local[0].start()
    barrier = pltpu.get_barrier_semaphore()

    def greet(peer):
        @pl.when(peer > me)
        def _():
            signal(barrier, peer)

    each(1, n, greet)
    for copy in local[1:]:
        copy.start()

    @pl.when(me > 0)
    def _():
        pl.semaphore_wait(barrier, me)

    def answer(peer):
        @pl.when(peer < me)
        def _():
            signal(ready.at[mine], peer)

    each(0, n - 1, answer)

    @pl.when(core == 1)
    def _():
        signal(paired, partner)
    local[0].wait()
    for h in range(H):
        rows32[h:h + 1] = flat_q[:, h * HD:(h + 1) * HD].astype(jnp.float32)
    q[...] = rows32[...].astype(jnp.bfloat16)
    qbuf[me] = q[own_half]

    def q_copy(peer):
        cut = pl.ds(pl.multiple_of(lax.rem(peer, 2) * HALF, HALF), HALF)
        return remote(q.at[cut], qbuf.at[me], q_send.at[peer], q_recv.at[me], peer)

    away_cols = pl.ds(pl.multiple_of((1 - core) * width, width), width)
    kv = [
        remote(k.at[:, away_cols], kbuf.at[pl.ds(rows, rows)], kv_send.at[0], kv_recv.at[0], partner),
        remote(v.at[:, away_cols], vbuf.at[pl.ds(rows, rows)], kv_send.at[1], kv_recv.at[1], partner),
    ]

    def ask(group):
        @pl.when(group > mine)
        def _():
            pl.semaphore_wait(ready.at[group], 4)

        @pl.when(jnp.logical_and(group == mine, lax.rem(me, 4) < 3))
        def _():
            pl.semaphore_wait(ready.at[group], 3 - lax.rem(me, 4))

        for j in range(4):
            peer = group * 4 + j

            @pl.when(peer != me)
            def _():
                q_copy(peer).start()

    pages, page = skb.shape[0], skb.shape[1]
    slots = pages * page

    def suffix(low, high):
        lane = lax.broadcasted_iota(jnp.int32, (1, slots), 1)
        at_page = lane // page
        position = lane - at_page * page
        for j in range(pages):
            position = position + jnp.where(at_page == tables[0, j], j * page, 0)
        live = position < lens[0]
        for h in range(low, high):
            cols = pl.ds(h * HD, HD)
            keys = skb[:, :, cols].reshape(slots, HD)
            values = svb[:, :, cols].reshape(slots, HD)
            part = pl.ds(h * G, G)
            scores = lax.dot_general(q[part], keys, NT, preferred_element_type=jnp.float32)
            scores = jnp.where(live, scores, -jnp.inf)
            top = jnp.max(scores, axis=1, keepdims=True)
            expos = jnp.exp((scores - top) * SCALE)
            total = jnp.sum(expos, axis=1, keepdims=True)
            num = jnp.dot(expos.astype(jnp.bfloat16), values, preferred_element_type=jnp.float32)
            osuf[part] = num / total
            lsuf[part] = jnp.broadcast_to(top * SCALE + jnp.log(total), (G, HD))

    @pl.when(core == 0)
    def _():
        pl.semaphore_wait(paired, 1)

    for copy in kv:
        copy.start()
    for group in range(4):
        ask(group)
    if nb > 4:
        pl.loop(4, nb)(ask)
    for copy in local[1:5]:
        copy.wait()
    suffix(0, KVH)
    lsuf[...] = lsuf[...].T

    for copy in local[5:]:
        copy.wait()
    for copy in kv:
        copy.wait_recv()

    def o_copy(peer):
        return remote(osend.at[peer], orecv.at[me], o_send.at[peer], o_recv.at[me], peer)

    def s_copy(peer):
        return remote(ssend.at[peer], srecv.at[me], s_send.at[peer], s_recv.at[me], peer)

    kept = [
        pltpu.make_async_copy(osend.at[me], orecv.at[me], own_sem.at[7]),
        pltpu.make_async_copy(ssend.at[me], srecv.at[me], own_sem.at[8]),
    ]
    wide = lax.broadcasted_iota(jnp.int32, (G, HD), 1)

    def spread(column):
        tile = jnp.zeros((G, HD), jnp.float32)
        for s in range(4):
            tile = jnp.where(wide == s, column[s * G:(s + 1) * G], tile)
        return tile

    def own_first(b):
        return jnp.where(b == 0, mine, jnp.where(b <= mine, b - 1, b))

    def turn(b):
        return own_first(jnp.where(jnp.logical_and(mine < nb - 2, b >= nb - 2), 2 * nb - 3 - b, b))

    def batch(b):
        group = turn(b)
        for j in range(4):
            source = group * 4 + j

            @pl.when(source != me)
            def _():
                remote(qbuf.at[source], qbuf.at[source], q_send.at[source], q_recv.at[source], partner).wait_recv()

        four = pl.ds(pl.multiple_of(group * 4, 4), 4)
        lses, steps = [], []
        ones = jnp.ones((kbuf.shape[0], HD), jnp.bfloat16)
        for h in range(HK):
            cols = pl.ds(h * HD, HD)
            asked = qbuf[four, pl.ds(h * G, G), :].reshape(4 * G, HD)
            scores = lax.dot_general(asked, kbuf[:, cols], NT, preferred_element_type=jnp.float32)
            top = jnp.max(scores, axis=1, keepdims=True)
            expos = jnp.exp((scores - top) * SCALE)
            wider = jnp.concatenate([vbuf[:, cols], ones], axis=1)
            both = jnp.dot(expos.astype(jnp.bfloat16), wider, preferred_element_type=jnp.float32)
            num, total = both[:, :HD], both[:, HD:]
            peak = jnp.maximum(jnp.max(jnp.abs(num), axis=1, keepdims=True), 1e-30)
            fixed = jnp.round(num * (FULL / peak)).astype(jnp.int32).astype(LINK)
            osend[four, pl.ds(h * G, G), :] = fixed.reshape(4, G, HD)
            lses.append(spread(top * SCALE + jnp.log(total)))
            steps.append(spread(peak / (FULL * total)))
        flat = jnp.concatenate(lses + steps, axis=0).T
        for s in range(4):
            ssend[group * 4 + s] = flat[s:s + 1]
        for j in range(4):
            peer = group * 4 + j

            @pl.when(peer != me)
            def _():
                s_copy(peer).start()
                o_copy(peer).start()

        @pl.when(group == mine)
        def _():
            for copy in kept:
                copy.start()

    each(0, nb, batch)

    def s_wait(source):
        @pl.when(source != me)
        def _():
            remote(ssend.at[source], srecv.at[source], s_send.at[source], s_recv.at[source], partner).wait_recv()

    def o_wait(source):
        @pl.when(source != me)
        def _():
            remote(osend.at[source], orecv.at[source], o_send.at[source], o_recv.at[source], partner).wait_recv()

    chips = n // 2 // 1
    lanes = lax.broadcasted_iota(jnp.int32, (chips, HD), 1) < HALF
    top = lsuf[0:1]
    total = jnp.ones((1, HD), jnp.float32)
    acc = osuf[...]
    for copy in kept:
        copy.wait()
    for step in range(1):
        groups = [jnp.where(mine >= nb // 2, lax.rem(b + nb // 2, nb), b) for b in range(step * nb // 1, (step + 1) * nb // 1)]
        sources = [group * 4 + j for group in groups for j in range(4)]
        for source in sources:
            s_wait(source)
        even = jnp.concatenate([srecv[source] for source in sources[::2]], axis=0)
        odd = jnp.concatenate([srecv[source] for source in sources[1::2]], axis=0)
        lse = jnp.where(lanes, even, pltpu.roll(odd, HALF, 1))
        steps = jnp.where(lanes, pltpu.roll(even, HALF, 1), odd)
        higher = jnp.maximum(top, jnp.max(lse, axis=0, keepdims=True))
        keep = jnp.exp(top - higher)
        weight = jnp.exp(lse - higher)
        total = total * keep + jnp.sum(weight, axis=0, keepdims=True)
        top = higher
        weight = weight * steps
        if step == 1 - 1:
            inverse = 1.0 / total
            keep = keep * inverse
            weight = weight * inverse
        turned = jnp.concatenate([weight, keep, jnp.zeros((7 - chips % 8, HD), jnp.float32)], axis=0).T
        acc = acc * turned[:, chips:chips + 1]
        for group in groups:
            for j in range(4):
                o_wait(group * 4 + j)
        for i in range(chips):
            both = pl.ds(pl.multiple_of(sources[2 * i], 2), 2)
            acc = acc + turned[:, i:i + 1] * orecv[both].reshape(H, HD).astype(jnp.float32)
    out[...] = acc.astype(jnp.bfloat16)

    for copy in kv:
        copy.wait_send()

    def left(peer):
        @pl.when(peer != me)
        def _():
            q_copy(peer).wait_send()
            o_copy(peer).wait_send()
            s_copy(peer).wait_send()

    each(0, n, left)


def per_device(n, queries, keys, values, suffix_keys, suffix_values, lengths, tables):
    rows = keys.shape[0]
    pages, page, width = suffix_keys.shape[1:]
    dma = pltpu.SemaphoreType.DMA
    hbm = pl.BlockSpec(memory_space=pltpu.HBM)
    vector = pl.BlockSpec(memory_space=pltpu.VMEM)
    out = pl.pallas_call(
        functools.partial(kernel, n),
        out_shape=pltpu.VMEM((H, HD), jnp.bfloat16),
        in_specs=[hbm] * 7,
        out_specs=vector,
        scratch_shapes=[
            pltpu.VMEM(queries.shape, jnp.bfloat16),
            pltpu.SMEM(lengths.shape, jnp.int32),
            pltpu.SMEM(tables.shape, jnp.int32),
            pltpu.VMEM((H, HD), jnp.bfloat16),
            pltpu.VMEM((H, HD), jnp.float32),
            pltpu.VMEM((n, HALF, HD), jnp.bfloat16),
            pltpu.VMEM((2 * rows, width // 2), jnp.bfloat16),
            pltpu.VMEM((2 * rows, width // 2), jnp.bfloat16),
            pltpu.VMEM((pages, page, width), jnp.bfloat16),
            pltpu.VMEM((pages, page, width), jnp.bfloat16),
            pltpu.VMEM((n, HALF, HD), LINK),
            pltpu.VMEM((n, HALF, HD), LINK),
            pltpu.VMEM((n, 1, HD), jnp.float32),
            pltpu.VMEM((n, 1, HD), jnp.float32),
            pltpu.VMEM((H, HD), jnp.float32),
            pltpu.VMEM((H, HD), jnp.float32),
            dma((n,)), dma((n,)), dma((n,)), dma((n,)), dma((n,)), dma((n,)),
            dma((2,)), dma((2,)), dma((9,)),
            pltpu.SemaphoreType.REGULAR((n // 4,)),
            pltpu.SemaphoreType.REGULAR,
        ],
        compiler_params=pltpu.CompilerParams(collective_id=0, has_side_effects=True),
        name="attend",
    )(queries, keys, values, suffix_keys, suffix_values, lengths, tables)
    return out.reshape(1, H * HD)


def solution(mesh):
    rows = P(("groups", "seq"), None)
    pages = P(("groups", "seq"), None, None, None)
    return jax.shard_map(
        functools.partial(per_device, mesh.shape["seq"]),
        mesh=mesh,
        in_specs=(rows, rows, rows, pages, pages, P(("groups", "seq")), rows),
        out_specs=rows,
        check_vma=False,
    )
```

```python
import functools
import math

import jax
import jax.numpy as jnp
from jax import lax
from jax.experimental import pallas as pl
from jax.experimental.pallas import tpu as pltpu
from jax.sharding import PartitionSpec as P

H = 128
KVH = 8
HD = 128
G = H // KVH
HALF = H // 2
HK = KVH // 2
PACK = HALF // 2
LOW = 0xFFFF
GRAIN = 2.0 ** 18
UNROLL = 16
FULL = 32767.0
SCALE = 1.0 / math.sqrt(HD)
NT = (((1,), (1,)), ((), ()))


def kernel(
    n, q_hbm, k, v, sk, sv, lens_hbm, tables_hbm, out,
    flat_q, lens, tables, q, rows32, qbuf, kbuf, vbuf, skb, svb, osend, orecv, osuf, lsuf,
    q_send, q_recv, o_send, o_recv, kv_send, kv_recv, own_sem, ready, paired,
):
    me = lax.axis_index("seq")
    core = lax.rem(me, 2)
    partner = me + 1 - 2 * core
    rows = k.shape[0]
    width = k.shape[1] // 2
    nb = n // 4
    mine = me // 4

    def remote(src, dst, send, recv, peer):
        return pltpu.make_async_remote_copy(
            src_ref=src, dst_ref=dst, send_sem=send, recv_sem=recv,
            device_id={"seq": peer}, device_id_type=pl.DeviceIdType.MESH,
        )

    def signal(semaphore, peer):
        pl.semaphore_signal(
            semaphore, inc=1, device_id={"seq": peer}, device_id_type=pl.DeviceIdType.MESH
        )

    def each(low, high, step):
        if n <= UNROLL:
            for i in range(low, high):
                step(i)
        else:
            pl.loop(low, high)(step)

    own_cols = pl.ds(pl.multiple_of(core * width, width), width)
    own_half = pl.ds(pl.multiple_of(core * HALF, HALF), HALF)
    local = [
        pltpu.make_async_copy(q_hbm, flat_q, own_sem.at[0]),
        pltpu.make_async_copy(lens_hbm, lens, own_sem.at[1]),
        pltpu.make_async_copy(tables_hbm, tables, own_sem.at[2]),
        pltpu.make_async_copy(sk.at[0], skb, own_sem.at[3]),
        pltpu.make_async_copy(sv.at[0], svb, own_sem.at[4]),
        pltpu.make_async_copy(k.at[:, own_cols], kbuf.at[pl.ds(0, rows)], own_sem.at[5]),
        pltpu.make_async_copy(v.at[:, own_cols], vbuf.at[pl.ds(0, rows)], own_sem.at[5]),
    ]
    local[0].start()
    barrier = pltpu.get_barrier_semaphore()

    def greet(peer):
        @pl.when(peer > me)
        def _():
            signal(barrier, peer)

    each(1, n, greet)
    for copy in local[1:]:
        copy.start()

    @pl.when(me > 0)
    def _():
        pl.semaphore_wait(barrier, me)

    def answer(peer):
        @pl.when(peer < me)
        def _():
            signal(ready.at[mine], peer)

    each(0, n - 1, answer)

    @pl.when(core == 1)
    def _():
        signal(paired, partner)
    local[0].wait()
    for h in range(H):
        rows32[h:h + 1] = flat_q[:, h * HD:(h + 1) * HD].astype(jnp.float32)
    q[...] = rows32[...].astype(jnp.bfloat16)
    qbuf[me] = q[own_half]

    def q_copy(peer):
        cut = pl.ds(pl.multiple_of(lax.rem(peer, 2) * HALF, HALF), HALF)
        return remote(q.at[cut], qbuf.at[me], q_send, q_recv.at[me // 2], peer)

    away_cols = pl.ds(pl.multiple_of((1 - core) * width, width), width)
    kv = [
        remote(k.at[:, away_cols], kbuf.at[pl.ds(rows, rows)], kv_send, kv_recv, partner),
        remote(v.at[:, away_cols], vbuf.at[pl.ds(rows, rows)], kv_send, kv_recv, partner),
    ]

    def ask(group):
        @pl.when(group > mine)
        def _():
            pl.semaphore_wait(ready.at[group], 4)

        @pl.when(jnp.logical_and(group == mine, lax.rem(me, 4) < 3))
        def _():
            pl.semaphore_wait(ready.at[group], 3 - lax.rem(me, 4))

        for j in range(4):
            peer = group * 4 + j

            @pl.when(peer != me)
            def _():
                q_copy(peer).start()

    pages, page = skb.shape[0], skb.shape[1]
    slots = pages * page

    def suffix(low, high):
        lane = lax.broadcasted_iota(jnp.int32, (1, slots), 1)
        at_page = lane // page
        position = lane - at_page * page
        for j in range(pages):
            position = position + jnp.where(at_page == tables[0, j], j * page, 0)
        live = position < lens[0]
        for h in range(low, high, 2):
            tops, totals, grown = [], [], []
            for i in range(2):
                keys = skb[:, :, pl.ds((h + i) * HD, HD)].reshape(slots, HD)
                scores = lax.dot_general(
                    q[pl.ds((h + i) * G, G)], keys, NT, preferred_element_type=jnp.float32
                )
                scores = jnp.where(live, scores, -jnp.inf)
                top = jnp.max(scores, axis=1, keepdims=True)
                expos = jnp.exp((scores - top) * SCALE)
                tops.append(top)
                totals.append(jnp.sum(expos, axis=1, keepdims=True))
                grown.append(expos.astype(jnp.bfloat16))
            values = svb[:, :, pl.ds(h * HD, 2 * HD)].reshape(slots, 2 * HD)
            both = jnp.dot(
                jnp.concatenate(grown, axis=0), values, preferred_element_type=jnp.float32
            )
            for i in range(2):
                part = pl.ds((h + i) * G, G)
                osuf[part] = both[i * G:(i + 1) * G, i * HD:(i + 1) * HD] / totals[i]
                lsuf[part] = jnp.broadcast_to(tops[i] * SCALE + jnp.log(totals[i]), (G, HD))

    @pl.when(core == 0)
    def _():
        pl.semaphore_wait(paired, 1)

    for copy in kv:
        copy.start()
    for group in range(4):
        ask(group)
    if nb > 4:
        pl.loop(4, nb)(ask)
    for copy in local[1:5]:
        copy.wait()
    suffix(0, KVH)
    lsuf[...] = lsuf[...].T

    pltpu.make_async_copy(kbuf, kbuf, own_sem.at[5]).wait()
    both_kv = remote(kbuf, kbuf, kv_send, kv_recv, partner)
    both_kv.wait_recv()

    def o_copy(peer):
        return remote(osend.at[peer], orecv.at[me], o_send, o_recv, peer)

    kept = pltpu.make_async_copy(osend.at[me], orecv.at[me], own_sem.at[6])
    wide = lax.broadcasted_iota(jnp.int32, (G, HD), 1)

    def spread(column, count):
        tile = jnp.zeros((G, HD), jnp.float32)
        for s in range(count):
            tile = jnp.where(wide == s, column[s * G:(s + 1) * G], tile)
        return tile

    def own_first(b):
        return jnp.where(b == 0, mine, jnp.where(b <= mine, b - 1, b))

    def turn(b):
        return own_first(jnp.where(jnp.logical_and(mine < nb - 2, b >= nb - 2), 2 * nb - 3 - b, b))

    def batch(group, first, count):
        def arrived(sources, chip):
            remote(qbuf.at[sources], qbuf.at[sources], q_send, q_recv.at[chip], partner).wait_recv()

        for j in range(first, first + count, 2):
            chip = group * 2 + j // 2
            pl.when(chip == me // 2)(lambda: arrived(pl.ds(partner, 1), chip))
            pl.when(chip != me // 2)(lambda: arrived(pl.ds(2 * chip, 2), chip))

        some = pl.ds(pl.multiple_of(group * 4 + first, count), count)
        lses, steps, held_back = [], [], []
        ones = jnp.ones((kbuf.shape[0], HD), jnp.bfloat16)
        for h in range(HK):
            cols = pl.ds(h * HD, HD)
            asked = qbuf[some, pl.ds(h * G, G), :].reshape(count * G, HD)
            scores = lax.dot_general(asked, kbuf[:, cols], NT, preferred_element_type=jnp.float32)
            top = jnp.max(scores, axis=1, keepdims=True)
            expos = jnp.exp((scores - top) * SCALE)
            wider = jnp.concatenate([vbuf[:, cols], ones], axis=1)
            both = jnp.dot(expos.astype(jnp.bfloat16), wider, preferred_element_type=jnp.float32)
            num, total = both[:, :HD], both[:, HD:]
            peak = jnp.maximum(jnp.max(jnp.abs(num), axis=1, keepdims=True), 1e-30)
            fixed = jnp.round(num * (FULL / peak)).astype(jnp.int32)
            if h < HK // 2:
                held_back.append(fixed)
            else:
                fixed = (fixed << 16) | (held_back[h - HK // 2] & LOW)
                osend[some, pl.ds((h - HK // 2) * G, G), :] = fixed.reshape(count, G, HD)
            lses.append(spread(top * SCALE + jnp.log(total), count))
            steps.append(spread(jnp.log(peak / (FULL * total)), count))
        flat = jnp.concatenate(lses + steps, axis=0).T
        flat = jnp.round(flat[:8] * GRAIN).astype(jnp.int32)
        for s in range(count):
            osend[group * 4 + first + s, PACK:] = flat[s:s + 1]
        for j in range(first, first + count):
            peer = group * 4 + j

            @pl.when(peer != me)
            def _():
                o_copy(peer).start()

        own = lax.rem(me, 4)
        here = jnp.logical_and(own >= first, own < first + count)

        @pl.when(jnp.logical_and(group == mine, here))
        def _():
            kept.start()

    def serve(b):
        group = turn(b)
        early = jnp.logical_and(group == 0, mine >= nb // 2)

        @pl.when(early)
        def _():
            batch(group, 0, 2)
            batch(group, 2, 2)

        @pl.when(jnp.logical_not(early))
        def _():
            batch(group, 0, 4)

    pl.loop(0, nb)(serve)

    chips = n // 2 // 1
    lanes = lax.broadcasted_iota(jnp.int32, (chips, HD), 1) < HALF
    top = lsuf[0:1]
    total = jnp.ones((1, HD), jnp.float32)
    acc = osuf[...]
    kept.wait()
    others = pl.ds(0, n - 1)
    all_o = remote(osend.at[others], orecv.at[others], o_send, o_recv, partner)
    all_o.wait_recv()
    for step in range(1):
        groups = [b for b in range(step * nb // 1, (step + 1) * nb // 1)]
        sources = [group * 4 + j for group in groups for j in range(4)]
        even = jnp.concatenate([orecv[source, PACK:] for source in sources[::2]], axis=0)
        odd = jnp.concatenate([orecv[source, PACK:] for source in sources[1::2]], axis=0)
        even, odd = even.astype(jnp.float32) / GRAIN, odd.astype(jnp.float32) / GRAIN
        lse = jnp.where(lanes, even, pltpu.roll(odd, HALF, 1))
        steps = jnp.exp(jnp.where(lanes, pltpu.roll(even, HALF, 1), odd))
        higher = jnp.maximum(top, jnp.max(lse, axis=0, keepdims=True))
        keep = jnp.exp(top - higher)
        weight = jnp.exp(lse - higher)
        total = total * keep + jnp.sum(weight, axis=0, keepdims=True)
        top = higher
        weight = weight * steps
        if step == 1 - 1:
            inverse = 1.0 / total
            keep = keep * inverse
            weight = weight * inverse
        turned = jnp.concatenate([weight, keep, jnp.zeros((7 - chips % 8, HD), jnp.float32)], axis=0).T
        acc = acc * turned[:, chips:chips + 1]
        for i in range(chips):
            words = [orecv[source, :PACK] for source in sources[2 * i:2 * i + 2]]
            parts = [part for word in words for part in ((word << 16) >> 16, word >> 16)]
            acc = acc + turned[:, i:i + 1] * jnp.concatenate(parts, axis=0).astype(jnp.float32)
    out[...] = acc.astype(jnp.bfloat16)

    both_kv.wait_send()
    remote(qbuf.at[others], qbuf.at[others], q_send, q_recv.at[0], partner).wait_send()
    all_o.wait_send()


def per_device(n, queries, keys, values, suffix_keys, suffix_values, lengths, tables):
    rows = keys.shape[0]
    pages, page, width = suffix_keys.shape[1:]
    dma = pltpu.SemaphoreType.DMA
    hbm = pl.BlockSpec(memory_space=pltpu.HBM)
    vector = pl.BlockSpec(memory_space=pltpu.VMEM)
    out = pl.pallas_call(
        functools.partial(kernel, n),
        out_shape=pltpu.VMEM((H, HD), jnp.bfloat16),
        in_specs=[hbm] * 7,
        out_specs=vector,
        scratch_shapes=[
            pltpu.VMEM(queries.shape, jnp.bfloat16),
            pltpu.SMEM(lengths.shape, jnp.int32),
            pltpu.SMEM(tables.shape, jnp.int32),
            pltpu.VMEM((H, HD), jnp.bfloat16),
            pltpu.VMEM((H, HD), jnp.float32),
            pltpu.VMEM((n, HALF, HD), jnp.bfloat16),
            pltpu.VMEM((2 * rows, width // 2), jnp.bfloat16),
            pltpu.VMEM((2 * rows, width // 2), jnp.bfloat16),
            pltpu.VMEM((pages, page, width), jnp.bfloat16),
            pltpu.VMEM((pages, page, width), jnp.bfloat16),
            pltpu.VMEM((n, PACK + 1, HD), jnp.int32),
            pltpu.VMEM((n, PACK + 1, HD), jnp.int32),
            pltpu.VMEM((H, HD), jnp.float32),
            pltpu.VMEM((H, HD), jnp.float32),
            dma, dma((n // 2,)), dma, dma,
            dma, dma, dma((7,)),
            pltpu.SemaphoreType.REGULAR((n // 4,)),
            pltpu.SemaphoreType.REGULAR,
        ],
        compiler_params=pltpu.CompilerParams(collective_id=0, has_side_effects=True),
        name="attend",
    )(queries, keys, values, suffix_keys, suffix_values, lengths, tables)
    return out.reshape(1, H * HD)


def solution(mesh):
    rows = P(("groups", "seq"), None)
    pages = P(("groups", "seq"), None, None, None)
    return jax.shard_map(
        functools.partial(per_device, mesh.shape["seq"]),
        mesh=mesh,
        in_specs=(rows, rows, rows, pages, pages, P(("groups", "seq")), rows),
        out_specs=rows,
        check_vma=False,
    )
```

```python
import functools
import math

import jax
import jax.numpy as jnp
from jax import lax
from jax.experimental import pallas as pl
from jax.experimental.pallas import tpu as pltpu
from jax.sharding import PartitionSpec as P

H = 128
KVH = 8
HD = 128
G = H // KVH
HALF = H // 2
HK = KVH // 2
PACK = HALF // 2
LOW = 0xFFFF
GRAIN = 2.0 ** 18
UNROLL = 16
FULL = 32767.0
SCALE = 1.0 / math.sqrt(HD)
NT = (((1,), (1,)), ((), ()))


def kernel(
    n, q_hbm, k, v, sk, sv, lens_hbm, tables_hbm, out,
    flat_q, lens, tables, q, rows32, qbuf, kbuf, vbuf, skb, svb, osend, orecv, osuf, lsuf,
    q_send, q_recv, o_send, o_recv, kv_send, kv_recv, own_sem, ready, paired,
):
    me = lax.axis_index("seq")
    core = lax.rem(me, 2)
    partner = me + 1 - 2 * core
    rows = k.shape[0]
    width = k.shape[1] // 2
    nb = n // 4
    mine = me // 4

    def remote(src, dst, send, recv, peer):
        return pltpu.make_async_remote_copy(
            src_ref=src, dst_ref=dst, send_sem=send, recv_sem=recv,
            device_id={"seq": peer}, device_id_type=pl.DeviceIdType.MESH,
        )

    def signal(semaphore, peer):
        pl.semaphore_signal(
            semaphore, inc=1, device_id={"seq": peer}, device_id_type=pl.DeviceIdType.MESH
        )

    def each(low, high, step):
        if n <= UNROLL:
            for i in range(low, high):
                step(i)
        else:
            pl.loop(low, high)(step)

    own_cols = pl.ds(pl.multiple_of(core * width, width), width)
    own_half = pl.ds(pl.multiple_of(core * HALF, HALF), HALF)
    local = [
        pltpu.make_async_copy(q_hbm, flat_q, own_sem.at[0]),
        pltpu.make_async_copy(lens_hbm, lens, own_sem.at[1]),
        pltpu.make_async_copy(tables_hbm, tables, own_sem.at[2]),
        pltpu.make_async_copy(sk.at[0], skb, own_sem.at[3]),
        pltpu.make_async_copy(sv.at[0], svb, own_sem.at[4]),
        pltpu.make_async_copy(k.at[:, own_cols], kbuf.at[pl.ds(0, rows)], own_sem.at[5]),
        pltpu.make_async_copy(v.at[:, own_cols], vbuf.at[pl.ds(0, rows)], own_sem.at[5]),
    ]
    local[0].start()
    barrier = pltpu.get_barrier_semaphore()

    def greet(peer):
        @pl.when(peer > me)
        def _():
            signal(barrier, peer)

    each(1, n, greet)
    for copy in local[1:]:
        copy.start()

    @pl.when(me > 0)
    def _():
        pl.semaphore_wait(barrier, me)

    def answer(peer):
        @pl.when(peer < me)
        def _():
            signal(ready.at[mine], peer)

    each(0, n - 1, answer)

    @pl.when(core == 1)
    def _():
        signal(paired, partner)
    local[0].wait()
    for h in range(H):
        rows32[h:h + 1] = flat_q[:, h * HD:(h + 1) * HD].astype(jnp.float32)
    q[...] = rows32[...].astype(jnp.bfloat16)
    qbuf[me] = q[own_half]

    def q_copy(peer):
        cut = pl.ds(pl.multiple_of(lax.rem(peer, 2) * HALF, HALF), HALF)
        return remote(q.at[cut], qbuf.at[me], q_send, q_recv.at[me // 2], peer)

    away_cols = pl.ds(pl.multiple_of((1 - core) * width, width), width)
    kv = [
        remote(k.at[:, away_cols], kbuf.at[pl.ds(rows, rows)], kv_send, kv_recv, partner),
        remote(v.at[:, away_cols], vbuf.at[pl.ds(rows, rows)], kv_send, kv_recv, partner),
    ]

    def ask(group):
        @pl.when(group > mine)
        def _():
            pl.semaphore_wait(ready.at[group], 4)

        @pl.when(jnp.logical_and(group == mine, lax.rem(me, 4) < 3))
        def _():
            pl.semaphore_wait(ready.at[group], 3 - lax.rem(me, 4))

        for j in range(4):
            peer = group * 4 + j

            @pl.when(peer != me)
            def _():
                q_copy(peer).start()

    pages, page = skb.shape[0], skb.shape[1]
    slots = pages * page

    def suffix(low, high):
        lane = lax.broadcasted_iota(jnp.int32, (1, slots), 1)
        at_page = lane // page
        position = lane - at_page * page
        for j in range(pages):
            position = position + jnp.where(at_page == tables[0, j], j * page, 0)
        live = position < lens[0]
        for h in range(low, high, 2):
            tops, totals, grown = [], [], []
            for i in range(2):
                keys = skb[:, :, pl.ds((h + i) * HD, HD)].reshape(slots, HD)
                scores = lax.dot_general(
                    q[pl.ds((h + i) * G, G)], keys, NT, preferred_element_type=jnp.float32
                )
                scores = jnp.where(live, scores, -jnp.inf)
                top = jnp.max(scores, axis=1, keepdims=True)
                expos = jnp.exp((scores - top) * SCALE)
                tops.append(top)
                totals.append(jnp.sum(expos, axis=1, keepdims=True))
                grown.append(expos.astype(jnp.bfloat16))
            values = svb[:, :, pl.ds(h * HD, 2 * HD)].reshape(slots, 2 * HD)
            both = jnp.dot(
                jnp.concatenate(grown, axis=0), values, preferred_element_type=jnp.float32
            )
            for i in range(2):
                part = pl.ds((h + i) * G, G)
                osuf[part] = both[i * G:(i + 1) * G, i * HD:(i + 1) * HD] / totals[i]
                lsuf[part] = jnp.broadcast_to(tops[i] * SCALE + jnp.log(totals[i]), (G, HD))

    @pl.when(core == 0)
    def _():
        pl.semaphore_wait(paired, 1)

    for copy in kv:
        copy.start()
    for group in range(4):
        ask(group)
    if nb > 4:
        pl.loop(4, nb)(ask)
    for copy in local[1:5]:
        copy.wait()
    suffix(0, KVH)
    lsuf[...] = lsuf[...].T

    pltpu.make_async_copy(kbuf, kbuf, own_sem.at[5]).wait()
    both_kv = remote(kbuf, kbuf, kv_send, kv_recv, partner)
    both_kv.wait_recv()

    def o_copy(peer):
        return remote(osend.at[peer], orecv.at[me], o_send, o_recv, peer)

    kept = pltpu.make_async_copy(osend.at[me], orecv.at[me], own_sem.at[6])
    wide = lax.broadcasted_iota(jnp.int32, (G, HD), 1)

    def spread(column, count):
        tile = jnp.zeros((G, HD), jnp.float32)
        for s in range(count):
            tile = jnp.where(wide == s, column[s * G:(s + 1) * G], tile)
        return tile

    def own_first(b):
        return jnp.where(b == 0, mine, jnp.where(b <= mine, b - 1, b))

    def turn(b):
        return jnp.where(mine == nb - 1, own_first(jnp.where(b == 0, 0, jnp.where(b == 1, nb - 1, jnp.where(b == 2, 1, b - 1)))), own_first(jnp.where(jnp.logical_and(mine < nb - 2, b >= nb - 2), 2 * nb - 3 - b, b)))

    def batch(group, first, count):
        def arrived(sources, chip):
            remote(qbuf.at[sources], qbuf.at[sources], q_send, q_recv.at[chip], partner).wait_recv()

        for j in range(first, first + count, 2):
            chip = group * 2 + j // 2
            pl.when(chip == me // 2)(lambda: arrived(pl.ds(partner, 1), chip))
            pl.when(chip != me // 2)(lambda: arrived(pl.ds(2 * chip, 2), chip))

        some = pl.ds(pl.multiple_of(group * 4 + first, count), count)
        lses, steps, held_back = [], [], []
        ones = jnp.ones((kbuf.shape[0], HD), jnp.bfloat16)
        for h in range(HK):
            cols = pl.ds(h * HD, HD)
            asked = qbuf[some, pl.ds(h * G, G), :].reshape(count * G, HD)
            scores = lax.dot_general(asked, kbuf[:, cols], NT, preferred_element_type=jnp.float32)
            top = jnp.max(scores, axis=1, keepdims=True)
            expos = jnp.exp((scores - top) * SCALE)
            wider = jnp.concatenate([vbuf[:, cols], ones], axis=1)
            both = jnp.dot(expos.astype(jnp.bfloat16), wider, preferred_element_type=jnp.float32)
            num, total = both[:, :HD], both[:, HD:]
            peak = jnp.maximum(jnp.max(jnp.abs(num), axis=1, keepdims=True), 1e-30)
            fixed = jnp.round(num * (FULL / peak)).astype(jnp.int32)
            if h < HK // 2:
                held_back.append(fixed)
            else:
                fixed = (fixed << 16) | (held_back[h - HK // 2] & LOW)
                osend[some, pl.ds((h - HK // 2) * G, G), :] = fixed.reshape(count, G, HD)
            lses.append(spread(top * SCALE + jnp.log(total), count))
            steps.append(spread(jnp.log(peak / (FULL * total)), count))
        flat = jnp.concatenate(lses + steps, axis=0).T
        flat = jnp.round(flat[:8] * GRAIN).astype(jnp.int32)
        for s in range(count):
            osend[group * 4 + first + s, PACK:] = flat[s:s + 1]
        for j in range(count):
            peer = group * 4 + first + jnp.where(group > 0, j + 1 - 2 * (j % 2), j)

            @pl.when(peer != me)
            def _():
                o_copy(peer).start()

        own = lax.rem(me, 4)
        here = jnp.logical_and(own >= first, own < first + count)

        @pl.when(jnp.logical_and(group == mine, here))
        def _():
            kept.start()

    def serve(b):
        group = turn(b)
        early = jnp.logical_and(group == 0, mine == nb - 1)

        @pl.when(early)
        def _():
            batch(group, 0, 2)
            batch(group, 2, 2)

        @pl.when(jnp.logical_not(early))
        def _():
            batch(group, 0, 4)

    pl.loop(0, nb)(serve)

    chips = n // 2 // 1
    lanes = lax.broadcasted_iota(jnp.int32, (chips, HD), 1) < HALF
    top = lsuf[0:1]
    total = jnp.ones((1, HD), jnp.float32)
    acc = osuf[...]
    kept.wait()
    others = pl.ds(0, n - 1)
    all_o = remote(osend.at[others], orecv.at[others], o_send, o_recv, partner)
    all_o.wait_recv()
    for step in range(1):
        groups = [b for b in range(step * nb // 1, (step + 1) * nb // 1)]
        sources = [group * 4 + j for group in groups for j in range(4)]
        even = jnp.concatenate([orecv[source, PACK:] for source in sources[::2]], axis=0)
        odd = jnp.concatenate([orecv[source, PACK:] for source in sources[1::2]], axis=0)
        even, odd = even.astype(jnp.float32) / GRAIN, odd.astype(jnp.float32) / GRAIN
        lse = jnp.where(lanes, even, pltpu.roll(odd, HALF, 1))
        steps = jnp.exp(jnp.where(lanes, pltpu.roll(even, HALF, 1), odd))
        higher = jnp.maximum(top, jnp.max(lse, axis=0, keepdims=True))
        keep = jnp.exp(top - higher)
        weight = jnp.exp(lse - higher)
        total = total * keep + jnp.sum(weight, axis=0, keepdims=True)
        top = higher
        weight = weight * steps
        if step == 1 - 1:
            inverse = 1.0 / total
            keep = keep * inverse
            weight = weight * inverse
        turned = jnp.concatenate([weight, keep, jnp.zeros((7 - chips % 8, HD), jnp.float32)], axis=0).T
        acc = acc * turned[:, chips:chips + 1]
        for i in range(chips):
            words = [orecv[source, :PACK] for source in sources[2 * i:2 * i + 2]]
            parts = [part for word in words for part in ((word << 16) >> 16, word >> 16)]
            acc = acc + turned[:, i:i + 1] * jnp.concatenate(parts, axis=0).astype(jnp.float32)
    out[...] = acc.astype(jnp.bfloat16)

    both_kv.wait_send()
    remote(qbuf.at[others], qbuf.at[others], q_send, q_recv.at[0], partner).wait_send()
    all_o.wait_send()


def per_device(n, queries, keys, values, suffix_keys, suffix_values, lengths, tables):
    rows = keys.shape[0]
    pages, page, width = suffix_keys.shape[1:]
    dma = pltpu.SemaphoreType.DMA
    hbm = pl.BlockSpec(memory_space=pltpu.HBM)
    vector = pl.BlockSpec(memory_space=pltpu.VMEM)
    out = pl.pallas_call(
        functools.partial(kernel, n),
        out_shape=pltpu.VMEM((H, HD), jnp.bfloat16),
        in_specs=[hbm] * 7,
        out_specs=vector,
        scratch_shapes=[
            pltpu.VMEM(queries.shape, jnp.bfloat16),
            pltpu.SMEM(lengths.shape, jnp.int32),
            pltpu.SMEM(tables.shape, jnp.int32),
            pltpu.VMEM((H, HD), jnp.bfloat16),
            pltpu.VMEM((H, HD), jnp.float32),
            pltpu.VMEM((n, HALF, HD), jnp.bfloat16),
            pltpu.VMEM((2 * rows, width // 2), jnp.bfloat16),
            pltpu.VMEM((2 * rows, width // 2), jnp.bfloat16),
            pltpu.VMEM((pages, page, width), jnp.bfloat16),
            pltpu.VMEM((pages, page, width), jnp.bfloat16),
            pltpu.VMEM((n, PACK + 1, HD), jnp.int32),
            pltpu.VMEM((n, PACK + 1, HD), jnp.int32),
            pltpu.VMEM((H, HD), jnp.float32),
            pltpu.VMEM((H, HD), jnp.float32),
            dma, dma((n // 2,)), dma, dma,
            dma, dma, dma((7,)),
            pltpu.SemaphoreType.REGULAR((n // 4,)),
            pltpu.SemaphoreType.REGULAR,
        ],
        compiler_params=pltpu.CompilerParams(collective_id=0, has_side_effects=True),
        name="attend",
    )(queries, keys, values, suffix_keys, suffix_values, lengths, tables)
    return out.reshape(1, H * HD)


def solution(mesh):
    rows = P(("groups", "seq"), None)
    pages = P(("groups", "seq"), None, None, None)
    return jax.shard_map(
        functools.partial(per_device, mesh.shape["seq"]),
        mesh=mesh,
        in_specs=(rows, rows, rows, pages, pages, P(("groups", "seq")), rows),
        out_specs=rows,
        check_vma=False,
    )
```

```python
import functools
import math

import jax
import jax.numpy as jnp
from jax import lax
from jax.experimental import pallas as pl
from jax.experimental.pallas import tpu as pltpu
from jax.sharding import PartitionSpec as P

H = 128
KVH = 8
HD = 128
G = H // KVH
HALF = H // 2
HK = KVH // 2
PACK = HALF // 2
LOW = 0xFFFF
GRAIN = 2.0 ** 18
UNROLL = 16
FULL = 32767.0
SCALE = 1.0 / math.sqrt(HD)
NT = (((1,), (1,)), ((), ()))


def kernel(
    n, q_hbm, k, v, sk, sv, lens_hbm, tables_hbm, out,
    flat_q, lens, tables, q, rows32, qbuf, kbuf, vbuf, skb, svb, osend, orecv, osuf, lsuf,
    q_send, q_recv, o_send, o_recv, kv_send, kv_recv, own_sem, ready, paired,
):
    me = lax.axis_index("seq")
    core = lax.rem(me, 2)
    partner = me + 1 - 2 * core
    rows = k.shape[0]
    width = k.shape[1] // 2
    nb = n // 4
    mine = me // 4

    def remote(src, dst, send, recv, peer):
        return pltpu.make_async_remote_copy(
            src_ref=src, dst_ref=dst, send_sem=send, recv_sem=recv,
            device_id={"seq": peer}, device_id_type=pl.DeviceIdType.MESH,
        )

    def signal(semaphore, peer):
        pl.semaphore_signal(
            semaphore, inc=1, device_id={"seq": peer}, device_id_type=pl.DeviceIdType.MESH
        )

    def each(low, high, step):
        if n <= UNROLL:
            for i in range(low, high):
                step(i)
        else:
            pl.loop(low, high)(step)

    own_cols = pl.ds(pl.multiple_of(core * width, width), width)
    own_half = pl.ds(pl.multiple_of(core * HALF, HALF), HALF)
    local = [
        pltpu.make_async_copy(q_hbm, flat_q, own_sem.at[0]),
        pltpu.make_async_copy(lens_hbm, lens, own_sem.at[1]),
        pltpu.make_async_copy(tables_hbm, tables, own_sem.at[2]),
        pltpu.make_async_copy(sk.at[0], skb, own_sem.at[3]),
        pltpu.make_async_copy(sv.at[0], svb, own_sem.at[4]),
        pltpu.make_async_copy(k.at[:, own_cols], kbuf.at[pl.ds(0, rows)], own_sem.at[5]),
        pltpu.make_async_copy(v.at[:, own_cols], vbuf.at[pl.ds(0, rows)], own_sem.at[5]),
    ]
    local[0].start()
    barrier = pltpu.get_barrier_semaphore()

    def greet(peer):
        @pl.when(peer > me)
        def _():
            signal(barrier, peer)

    each(1, n, greet)
    for copy in local[1:]:
        copy.start()

    @pl.when(me > 0)
    def _():
        pl.semaphore_wait(barrier, me)

    def answer(peer):
        @pl.when(peer < me)
        def _():
            signal(ready.at[mine], peer)

    each(0, n - 1, answer)

    @pl.when(core == 1)
    def _():
        signal(paired, partner)
    local[0].wait()
    for h in range(H):
        rows32[h:h + 1] = flat_q[:, h * HD:(h + 1) * HD].astype(jnp.float32)
    q[...] = rows32[...].astype(jnp.bfloat16)
    qbuf[me] = q[own_half]

    def q_copy(peer):
        cut = pl.ds(pl.multiple_of(lax.rem(peer, 2) * HALF, HALF), HALF)
        return remote(q.at[cut], qbuf.at[me], q_send, q_recv.at[me // 2], peer)

    away_cols = pl.ds(pl.multiple_of((1 - core) * width, width), width)
    kv = [
        remote(k.at[:, away_cols], kbuf.at[pl.ds(rows, rows)], kv_send, kv_recv, partner),
        remote(v.at[:, away_cols], vbuf.at[pl.ds(rows, rows)], kv_send, kv_recv, partner),
    ]

    def ask(group):
        @pl.when(group > mine)
        def _():
            pl.semaphore_wait(ready.at[group], 4)

        @pl.when(jnp.logical_and(group == mine, lax.rem(me, 4) < 3))
        def _():
            pl.semaphore_wait(ready.at[group], 3 - lax.rem(me, 4))

        for j in range(4):
            peer = group * 4 + j

            @pl.when(peer != me)
            def _():
                q_copy(peer).start()

    pages, page = skb.shape[0], skb.shape[1]
    slots = pages * page

    def suffix(low, high):
        lane = lax.broadcasted_iota(jnp.int32, (1, slots), 1)
        at_page = lane // page
        position = lane - at_page * page
        for j in range(pages):
            position = position + jnp.where(at_page == tables[0, j], j * page, 0)
        live = position < lens[0]
        for h in range(low, high, 2):
            tops, totals, grown = [], [], []
            for i in range(2):
                keys = skb[:, :, pl.ds((h + i) * HD, HD)].reshape(slots, HD)
                scores = lax.dot_general(
                    q[pl.ds((h + i) * G, G)], keys, NT, preferred_element_type=jnp.float32
                )
                scores = jnp.where(live, scores, -jnp.inf)
                top = jnp.max(scores, axis=1, keepdims=True)
                expos = jnp.exp((scores - top) * SCALE)
                tops.append(top)
                totals.append(jnp.sum(expos, axis=1, keepdims=True))
                grown.append(expos.astype(jnp.bfloat16))
            values = svb[:, :, pl.ds(h * HD, 2 * HD)].reshape(slots, 2 * HD)
            both = jnp.dot(
                jnp.concatenate(grown, axis=0), values, preferred_element_type=jnp.float32
            )
            for i in range(2):
                part = pl.ds((h + i) * G, G)
                osuf[part] = both[i * G:(i + 1) * G, i * HD:(i + 1) * HD] / totals[i]
                lsuf[part] = jnp.broadcast_to(tops[i] * SCALE + jnp.log(totals[i]), (G, HD))

    @pl.when(core == 0)
    def _():
        pl.semaphore_wait(paired, 1)

    for copy in kv:
        copy.start()
    for group in range(4):
        ask(group)
    if nb > 4:
        pl.loop(4, nb)(ask)
    for copy in local[1:5]:
        copy.wait()
    suffix(0, KVH)
    lsuf[...] = lsuf[...].T

    pltpu.make_async_copy(kbuf, kbuf, own_sem.at[5]).wait()
    both_kv = remote(kbuf, kbuf, kv_send, kv_recv, partner)
    both_kv.wait_recv()

    def o_copy(peer):
        return remote(osend.at[peer], orecv.at[me], o_send, o_recv, peer)

    kept = pltpu.make_async_copy(osend.at[me], orecv.at[me], own_sem.at[6])
    wide = lax.broadcasted_iota(jnp.int32, (G, HD), 1)

    def spread(column, count):
        tile = jnp.zeros((G, HD), jnp.float32)
        for s in range(count):
            tile = jnp.where(wide == s, column[s * G:(s + 1) * G], tile)
        return tile

    def own_first(b):
        return jnp.where(b == 0, mine, jnp.where(b <= mine, b - 1, b))

    def turn(b):
        return jnp.where(jnp.logical_and(mine == 1, b < 2), 1 - b, jnp.where(mine == nb - 1, own_first(jnp.where(b == 0, 0, jnp.where(b == 1, nb - 1, jnp.where(b == 2, 1, b - 1)))), own_first(jnp.where(jnp.logical_and(mine < nb - 2, b >= nb - 2), 2 * nb - 3 - b, b))))

    def batch(group, first, count):
        def arrived(sources, chip):
            remote(qbuf.at[sources], qbuf.at[sources], q_send, q_recv.at[chip], partner).wait_recv()

        for j in range(first, first + count, 2):
            chip = group * 2 + j // 2
            pl.when(chip == me // 2)(lambda: arrived(pl.ds(partner, 1), chip))
            pl.when(chip != me // 2)(lambda: arrived(pl.ds(2 * chip, 2), chip))

        some = pl.ds(pl.multiple_of(group * 4 + first, count), count)
        lses, steps, held_back = [], [], []
        ones = jnp.ones((kbuf.shape[0], HD), jnp.bfloat16)
        for h in range(HK):
            cols = pl.ds(h * HD, HD)
            asked = qbuf[some, pl.ds(h * G, G), :].reshape(count * G, HD)
            scores = lax.dot_general(asked, kbuf[:, cols], NT, preferred_element_type=jnp.float32)
            top = jnp.max(scores, axis=1, keepdims=True)
            expos = jnp.exp((scores - top) * SCALE)
            wider = jnp.concatenate([vbuf[:, cols], ones], axis=1)
            both = jnp.dot(expos.astype(jnp.bfloat16), wider, preferred_element_type=jnp.float32)
            num, total = both[:, :HD], both[:, HD:]
            peak = jnp.maximum(jnp.max(jnp.abs(num), axis=1, keepdims=True), 1e-30)
            fixed = jnp.round(num * (FULL / peak)).astype(jnp.int32)
            if h < HK // 2:
                held_back.append(fixed)
            else:
                fixed = (fixed << 16) | (held_back[h - HK // 2] & LOW)
                osend[some, pl.ds((h - HK // 2) * G, G), :] = fixed.reshape(count, G, HD)
            lses.append(spread(top * SCALE + jnp.log(total), count))
            steps.append(spread(jnp.log(peak / (FULL * total)), count))
        flat = jnp.concatenate(lses + steps, axis=0).T
        flat = jnp.round(flat[:8] * GRAIN).astype(jnp.int32)
        for s in range(count):
            osend[group * 4 + first + s, PACK:] = flat[s:s + 1]
        for j in range(count):
            peer = group * 4 + first + jnp.where(jnp.logical_and(group > 0, core == 1), j + 1 - 2 * (j % 2), j)

            @pl.when(peer != me)
            def _():
                o_copy(peer).start()

        own = lax.rem(me, 4)
        here = jnp.logical_and(own >= first, own < first + count)

        @pl.when(jnp.logical_and(group == mine, here))
        def _():
            kept.start()

    def serve(b):
        group = turn(b)
        early = jnp.logical_and(group == 0, mine == nb - 1)

        @pl.when(early)
        def _():
            batch(group, 0, 2)
            batch(group, 2, 2)

        @pl.when(jnp.logical_not(early))
        def _():
            batch(group, 0, 4)

    pl.loop(0, nb)(serve)

    chips = n // 2 // 1
    lanes = lax.broadcasted_iota(jnp.int32, (chips, HD), 1) < HALF
    top = lsuf[0:1]
    total = jnp.ones((1, HD), jnp.float32)
    acc = osuf[...]
    kept.wait()
    others = pl.ds(0, n - 1)
    all_o = remote(osend.at[others], orecv.at[others], o_send, o_recv, partner)
    all_o.wait_recv()
    for step in range(1):
        groups = [b for b in range(step * nb // 1, (step + 1) * nb // 1)]
        sources = [group * 4 + j for group in groups for j in range(4)]
        even = jnp.concatenate([orecv[source, PACK:] for source in sources[::2]], axis=0)
        odd = jnp.concatenate([orecv[source, PACK:] for source in sources[1::2]], axis=0)
        even, odd = even.astype(jnp.float32) / GRAIN, odd.astype(jnp.float32) / GRAIN
        lse = jnp.where(lanes, even, pltpu.roll(odd, HALF, 1))
        steps = jnp.exp(jnp.where(lanes, pltpu.roll(even, HALF, 1), odd))
        higher = jnp.maximum(top, jnp.max(lse, axis=0, keepdims=True))
        keep = jnp.exp(top - higher)
        weight = jnp.exp(lse - higher)
        total = total * keep + jnp.sum(weight, axis=0, keepdims=True)
        top = higher
        weight = weight * steps
        if step == 1 - 1:
            inverse = 1.0 / total
            keep = keep * inverse
            weight = weight * inverse
        turned = jnp.concatenate([weight, keep, jnp.zeros((7 - chips % 8, HD), jnp.float32)], axis=0).T
        acc = acc * turned[:, chips:chips + 1]
        for i in range(chips):
            words = [orecv[source, :PACK] for source in sources[2 * i:2 * i + 2]]
            parts = [part for word in words for part in ((word << 16) >> 16, word >> 16)]
            acc = acc + turned[:, i:i + 1] * jnp.concatenate(parts, axis=0).astype(jnp.float32)
    for h in range(H):
        out[:, h * HD:(h + 1) * HD] = acc[h:h + 1].astype(jnp.bfloat16)

    both_kv.wait_send()
    remote(qbuf.at[others], qbuf.at[others], q_send, q_recv.at[0], partner).wait_send()
    all_o.wait_send()


def per_device(n, queries, keys, values, suffix_keys, suffix_values, lengths, tables):
    rows = keys.shape[0]
    pages, page, width = suffix_keys.shape[1:]
    dma = pltpu.SemaphoreType.DMA
    hbm = pl.BlockSpec(memory_space=pltpu.HBM)
    vector = pl.BlockSpec(memory_space=pltpu.VMEM)
    out = pl.pallas_call(
        functools.partial(kernel, n),
        out_shape=pltpu.VMEM((1, H * HD), jnp.bfloat16),
        in_specs=[hbm] * 7,
        out_specs=vector,
        scratch_shapes=[
            pltpu.VMEM(queries.shape, jnp.bfloat16),
            pltpu.SMEM(lengths.shape, jnp.int32),
            pltpu.SMEM(tables.shape, jnp.int32),
            pltpu.VMEM((H, HD), jnp.bfloat16),
            pltpu.VMEM((H, HD), jnp.float32),
            pltpu.VMEM((n, HALF, HD), jnp.bfloat16),
            pltpu.VMEM((2 * rows, width // 2), jnp.bfloat16),
            pltpu.VMEM((2 * rows, width // 2), jnp.bfloat16),
            pltpu.VMEM((pages, page, width), jnp.bfloat16),
            pltpu.VMEM((pages, page, width), jnp.bfloat16),
            pltpu.VMEM((n, PACK + 1, HD), jnp.int32),
            pltpu.VMEM((n, PACK + 1, HD), jnp.int32),
            pltpu.VMEM((H, HD), jnp.float32),
            pltpu.VMEM((H, HD), jnp.float32),
            dma, dma((n // 2,)), dma, dma,
            dma, dma, dma((7,)),
            pltpu.SemaphoreType.REGULAR((n // 4,)),
            pltpu.SemaphoreType.REGULAR,
        ],
        compiler_params=pltpu.CompilerParams(collective_id=0, has_side_effects=True),
        name="attend",
    )(queries, keys, values, suffix_keys, suffix_values, lengths, tables)
    return out


def solution(mesh):
    rows = P(("groups", "seq"), None)
    pages = P(("groups", "seq"), None, None, None)
    return jax.shard_map(
        functools.partial(per_device, mesh.shape["seq"]),
        mesh=mesh,
        in_specs=(rows, rows, rows, pages, pages, P(("groups", "seq")), rows),
        out_specs=rows,
        check_vma=False,
    )
```

```python
import functools
import math

import jax
import jax.numpy as jnp
from jax import lax
from jax.experimental import pallas as pl
from jax.experimental.pallas import tpu as pltpu
from jax.sharding import PartitionSpec as P

H = 128
KVH = 8
HD = 128
G = H // KVH
HALF = H // 2
HK = KVH // 2
PACK = HALF // 2
LOW = 0xFFFF
GRAIN = 2.0 ** 18
UNROLL = 16
FULL = 32767.0
SCALE = 1.0 / math.sqrt(HD)
NT = (((1,), (1,)), ((), ()))


def kernel(
    n, q_hbm, k, v, sk, sv, lens_hbm, tables_hbm, out,
    flat_q, lens, tables, q, rows32, qbuf, kbuf, vbuf, skb, svb, osend, orecv, osuf, lsuf,
    q_send, q_recv, o_send, o_recv, kv_send, kv_recv, own_sem, ready, paired,
):
    me = lax.axis_index("seq")
    core = lax.rem(me, 2)
    partner = me + 1 - 2 * core
    rows = k.shape[0]
    width = k.shape[1] // 2
    nb = n // 4
    mine = me // 4

    def remote(src, dst, send, recv, peer):
        return pltpu.make_async_remote_copy(
            src_ref=src, dst_ref=dst, send_sem=send, recv_sem=recv,
            device_id={"seq": peer}, device_id_type=pl.DeviceIdType.MESH,
        )

    def signal(semaphore, peer):
        pl.semaphore_signal(
            semaphore, inc=1, device_id={"seq": peer}, device_id_type=pl.DeviceIdType.MESH
        )

    def each(low, high, step):
        if n <= UNROLL:
            for i in range(low, high):
                step(i)
        else:
            pl.loop(low, high)(step)

    own_cols = pl.ds(pl.multiple_of(core * width, width), width)
    own_half = pl.ds(pl.multiple_of(core * HALF, HALF), HALF)
    local = [
        pltpu.make_async_copy(q_hbm, flat_q, own_sem.at[0]),
        pltpu.make_async_copy(lens_hbm, lens, own_sem.at[1]),
        pltpu.make_async_copy(tables_hbm, tables, own_sem.at[2]),
        pltpu.make_async_copy(sk.at[0], skb, own_sem.at[3]),
        pltpu.make_async_copy(sv.at[0], svb, own_sem.at[4]),
        pltpu.make_async_copy(k.at[:, own_cols], kbuf.at[pl.ds(0, rows)], own_sem.at[5]),
        pltpu.make_async_copy(v.at[:, own_cols], vbuf.at[pl.ds(0, rows)], own_sem.at[5]),
    ]
    local[0].start()
    barrier = pltpu.get_barrier_semaphore()

    def greet(peer):
        @pl.when(peer > me)
        def _():
            signal(barrier, peer)

    each(1, n, greet)
    for copy in local[1:]:
        copy.start()

    @pl.when(me > 0)
    def _():
        pl.semaphore_wait(barrier, me)

    def answer(peer):
        @pl.when(peer < me)
        def _():
            signal(ready.at[me // 2], peer)

    each(0, n - 1, answer)

    @pl.when(core == 1)
    def _():
        signal(paired, partner)
    local[0].wait()
    for h in range(H):
        rows32[h:h + 1] = flat_q[:, h * HD:(h + 1) * HD].astype(jnp.float32)
    q[...] = rows32[...].astype(jnp.bfloat16)
    qbuf[me] = q[own_half]

    def q_copy(peer):
        cut = pl.ds(pl.multiple_of(lax.rem(peer, 2) * HALF, HALF), HALF)
        return remote(q.at[cut], qbuf.at[me], q_send, q_recv.at[me // 2], peer)

    away_cols = pl.ds(pl.multiple_of((1 - core) * width, width), width)
    kv = [
        remote(k.at[:, away_cols], kbuf.at[pl.ds(rows, rows)], kv_send, kv_recv, partner),
        remote(v.at[:, away_cols], vbuf.at[pl.ds(rows, rows)], kv_send, kv_recv, partner),
    ]

    def ask(group):
        for j in range(4):
            peer = group * 4 + j
            chip = group * 2 + j // 2
            if j % 2 == 0:
                behind = jnp.logical_and(chip == me // 2, core == 0)
                pl.when(chip > me // 2)(lambda: pl.semaphore_wait(ready.at[chip], 2))
                pl.when(behind)(lambda: pl.semaphore_wait(ready.at[chip], 1))

            @pl.when(peer != me)
            def _():
                q_copy(peer).start()

    pages, page = skb.shape[0], skb.shape[1]
    slots = pages * page

    def suffix(low, high):
        lane = lax.broadcasted_iota(jnp.int32, (1, slots), 1)
        at_page = lane // page
        position = lane - at_page * page
        for j in range(pages):
            position = position + jnp.where(at_page == tables[0, j], j * page, 0)
        live = position < lens[0]
        for h in range(low, high, 2):
            tops, totals, grown = [], [], []
            for i in range(2):
                keys = skb[:, :, pl.ds((h + i) * HD, HD)].reshape(slots, HD)
                scores = lax.dot_general(
                    q[pl.ds((h + i) * G, G)], keys, NT, preferred_element_type=jnp.float32
                )
                scores = jnp.where(live, scores, -jnp.inf)
                top = jnp.max(scores, axis=1, keepdims=True)
                expos = jnp.exp((scores - top) * SCALE)
                tops.append(top)
                totals.append(jnp.sum(expos, axis=1, keepdims=True))
                grown.append(expos.astype(jnp.bfloat16))
            values = svb[:, :, pl.ds(h * HD, 2 * HD)].reshape(slots, 2 * HD)
            both = jnp.dot(
                jnp.concatenate(grown, axis=0), values, preferred_element_type=jnp.float32
            )
            for i in range(2):
                part = pl.ds((h + i) * G, G)
                osuf[part] = both[i * G:(i + 1) * G, i * HD:(i + 1) * HD] / totals[i]
                lsuf[part] = jnp.broadcast_to(tops[i] * SCALE + jnp.log(totals[i]), (G, HD))

    @pl.when(core == 0)
    def _():
        pl.semaphore_wait(paired, 1)

    for copy in kv:
        copy.start()
    for group in range(4):
        ask(group)
    if nb > 4:
        pl.loop(4, nb)(ask)
    for copy in local[1:5]:
        copy.wait()
    suffix(0, KVH)
    lsuf[...] = lsuf[...].T

    pltpu.make_async_copy(kbuf, kbuf, own_sem.at[5]).wait()
    both_kv = remote(kbuf, kbuf, kv_send, kv_recv, partner)
    both_kv.wait_recv()

    def o_copy(peer):
        return remote(osend.at[peer], orecv.at[me], o_send, o_recv, peer)

    kept = pltpu.make_async_copy(osend.at[me], orecv.at[me], own_sem.at[6])
    wide = lax.broadcasted_iota(jnp.int32, (G, HD), 1)

    def spread(column, count):
        tile = jnp.zeros((G, HD), jnp.float32)
        for s in range(count):
            tile = jnp.where(wide == s, column[s * G:(s + 1) * G], tile)
        return tile

    def own_first(b):
        return jnp.where(b == 0, mine, jnp.where(b <= mine, b - 1, b))

    def turn(b):
        return jnp.where(jnp.logical_and(mine == 1, b < 2), 1 - b, jnp.where(mine == nb - 1, own_first(jnp.where(b == 0, 0, jnp.where(b == 1, nb - 1, jnp.where(b == 2, 1, b - 1)))), own_first(jnp.where(jnp.logical_and(mine < nb - 2, b >= nb - 2), 2 * nb - 3 - b, b))))

    def batch(group, first, count):
        def arrived(sources, chip):
            remote(qbuf.at[sources], qbuf.at[sources], q_send, q_recv.at[chip], partner).wait_recv()

        for j in range(first, first + count, 2):
            chip = group * 2 + j // 2
            pl.when(chip == me // 2)(lambda: arrived(pl.ds(partner, 1), chip))
            pl.when(chip != me // 2)(lambda: arrived(pl.ds(2 * chip, 2), chip))

        some = pl.ds(pl.multiple_of(group * 4 + first, count), count)
        lses, steps, held_back = [], [], []
        ones = jnp.ones((kbuf.shape[0], HD), jnp.bfloat16)
        for h in range(HK):
            cols = pl.ds(h * HD, HD)
            asked = qbuf[some, pl.ds(h * G, G), :].reshape(count * G, HD)
            scores = lax.dot_general(asked, kbuf[:, cols], NT, preferred_element_type=jnp.float32)
            top = jnp.max(scores, axis=1, keepdims=True)
            expos = jnp.exp((scores - top) * SCALE)
            wider = jnp.concatenate([vbuf[:, cols], ones], axis=1)
            both = jnp.dot(expos.astype(jnp.bfloat16), wider, preferred_element_type=jnp.float32)
            num, total = both[:, :HD], both[:, HD:]
            peak = jnp.maximum(jnp.max(jnp.abs(num), axis=1, keepdims=True), 1e-30)
            fixed = jnp.round(num * (FULL / peak)).astype(jnp.int32)
            if h < HK // 2:
                held_back.append(fixed)
            else:
                fixed = (fixed << 16) | (held_back[h - HK // 2] & LOW)
                osend[some, pl.ds((h - HK // 2) * G, G), :] = fixed.reshape(count, G, HD)
            lses.append(spread(top * SCALE + jnp.log(total), count))
            steps.append(spread(jnp.log(peak / (FULL * total)), count))
        flat = jnp.concatenate(lses + steps, axis=0).T
        flat = jnp.round(flat[:8] * GRAIN).astype(jnp.int32)
        for s in range(count):
            osend[group * 4 + first + s, PACK:] = flat[s:s + 1]
        for j in range(count):
            peer = group * 4 + first + jnp.where(jnp.logical_and(group > 0, core == 1), j + 1 - 2 * (j % 2), j)

            @pl.when(peer != me)
            def _():
                o_copy(peer).start()

        own = lax.rem(me, 4)
        here = jnp.logical_and(own >= first, own < first + count)

        @pl.when(jnp.logical_and(group == mine, here))
        def _():
            kept.start()

    def serve(b):
        group = turn(b)
        early = jnp.logical_and(group == 0, mine == nb - 1)

        @pl.when(early)
        def _():
            batch(group, 0, 2)
            batch(group, 2, 2)

        @pl.when(jnp.logical_not(early))
        def _():
            batch(group, 0, 4)

    pl.loop(0, nb)(serve)

    chips = n // 2 // 1
    lanes = lax.broadcasted_iota(jnp.int32, (chips, HD), 1) < HALF
    top = lsuf[0:1]
    total = jnp.ones((1, HD), jnp.float32)
    acc = osuf[...]
    kept.wait()
    others = pl.ds(0, n - 1)
    all_o = remote(osend.at[others], orecv.at[others], o_send, o_recv, partner)
    all_o.wait_recv()
    for step in range(1):
        groups = [b for b in range(step * nb // 1, (step + 1) * nb // 1)]
        sources = [group * 4 + j for group in groups for j in range(4)]
        even = jnp.concatenate([orecv[source, PACK:] for source in sources[::2]], axis=0)
        odd = jnp.concatenate([orecv[source, PACK:] for source in sources[1::2]], axis=0)
        even, odd = even.astype(jnp.float32) / GRAIN, odd.astype(jnp.float32) / GRAIN
        lse = jnp.where(lanes, even, pltpu.roll(odd, HALF, 1))
        steps = jnp.exp(jnp.where(lanes, pltpu.roll(even, HALF, 1), odd))
        higher = jnp.maximum(top, jnp.max(lse, axis=0, keepdims=True))
        keep = jnp.exp(top - higher)
        weight = jnp.exp(lse - higher)
        total = total * keep + jnp.sum(weight, axis=0, keepdims=True)
        top = higher
        weight = weight * steps
        if step == 1 - 1:
            inverse = 1.0 / total
            keep = keep * inverse
            weight = weight * inverse
        turned = jnp.concatenate([weight, keep, jnp.zeros((7 - chips % 8, HD), jnp.float32)], axis=0).T
        acc = acc * turned[:, chips:chips + 1]
        for i in range(chips):
            words = [orecv[source, :PACK] for source in sources[2 * i:2 * i + 2]]
            parts = [part for word in words for part in ((word << 16) >> 16, word >> 16)]
            acc = acc + turned[:, i:i + 1] * jnp.concatenate(parts, axis=0).astype(jnp.float32)
    for h in range(H):
        out[:, h * HD:(h + 1) * HD] = acc[h:h + 1].astype(jnp.bfloat16)

    both_kv.wait_send()
    remote(qbuf.at[others], qbuf.at[others], q_send, q_recv.at[0], partner).wait_send()
    all_o.wait_send()


def per_device(n, queries, keys, values, suffix_keys, suffix_values, lengths, tables):
    rows = keys.shape[0]
    pages, page, width = suffix_keys.shape[1:]
    dma = pltpu.SemaphoreType.DMA
    hbm = pl.BlockSpec(memory_space=pltpu.HBM)
    vector = pl.BlockSpec(memory_space=pltpu.VMEM)
    out = pl.pallas_call(
        functools.partial(kernel, n),
        out_shape=pltpu.VMEM((1, H * HD), jnp.bfloat16),
        in_specs=[hbm] * 7,
        out_specs=vector,
        scratch_shapes=[
            pltpu.VMEM(queries.shape, jnp.bfloat16),
            pltpu.SMEM(lengths.shape, jnp.int32),
            pltpu.SMEM(tables.shape, jnp.int32),
            pltpu.VMEM((H, HD), jnp.bfloat16),
            pltpu.VMEM((H, HD), jnp.float32),
            pltpu.VMEM((n, HALF, HD), jnp.bfloat16),
            pltpu.VMEM((2 * rows, width // 2), jnp.bfloat16),
            pltpu.VMEM((2 * rows, width // 2), jnp.bfloat16),
            pltpu.VMEM((pages, page, width), jnp.bfloat16),
            pltpu.VMEM((pages, page, width), jnp.bfloat16),
            pltpu.VMEM((n, PACK + 1, HD), jnp.int32),
            pltpu.VMEM((n, PACK + 1, HD), jnp.int32),
            pltpu.VMEM((H, HD), jnp.float32),
            pltpu.VMEM((H, HD), jnp.float32),
            dma, dma((n // 2,)), dma, dma,
            dma, dma, dma((7,)),
            pltpu.SemaphoreType.REGULAR((n // 2,)),
            pltpu.SemaphoreType.REGULAR,
        ],
        compiler_params=pltpu.CompilerParams(collective_id=0, has_side_effects=True),
        name="attend",
    )(queries, keys, values, suffix_keys, suffix_values, lengths, tables)
    return out


def solution(mesh):
    rows = P(("groups", "seq"), None)
    pages = P(("groups", "seq"), None, None, None)
    return jax.shard_map(
        functools.partial(per_device, mesh.shape["seq"]),
        mesh=mesh,
        in_specs=(rows, rows, rows, pages, pages, P(("groups", "seq")), rows),
        out_specs=rows,
        check_vma=False,
    )
```
